32 devices in a mesh: groups: 2 (over y), row: 4 (over z), col: 2 (over x), chan: 2 (over core).
Axes of the slice: x: 2, y: 2, z: 4, core: 2. Of those that a mesh axis runs over, the one named last changes fastest.
Arguments:
- pair_input: bfloat16 [512, 256, 128], P(('groups', 'row'), ('col', 'chan')), parts along dimension 0, may hold values from -6 to 6
- alignment_features: bfloat16 [128, 512, 64], P('row', ('groups', 'col', 'chan')), parts along dimension 1, may hold values from -6 to 6
- alignment_mask: int32 [128, 512], P('row', ('groups', 'col', 'chan')), parts along dimension 1, may hold values from 0 to 1
- token_valid: int32 [512], P('groups'), parts along dimension 0, may hold values from 0 to 1, as said below
- left_weight: bfloat16 [64, 32], replicated, may hold values from -0.75 to 0.75
- right_weight: bfloat16 [64, 32], replicated, may hold values from -0.75 to 0.75
- output_weight: bfloat16 [1024, 128], replicated, may hold values from -1.75 to 1.75
- gate_weight: bfloat16 [128, 512], replicated, may hold values from -0.5 to 0.5
- up_weight: bfloat16 [128, 512], replicated, may hold values from -0.5 to 0.5
- down_weight: bfloat16 [512, 128], replicated, may hold values from -0.25 to 0.25
- kernel_weight: bfloat16 [3, 3, 128, 128], replicated, may hold values from -0.1875 to 0.1875
Outputs:
- pair_out: bfloat16 [512, 256, 128], P(('groups', 'row'), ('col', 'chan')), parts along dimension 0
The draws below stay inside these ranges and needn't reach their ends.
There are 2 independent parts, one for each index of `groups`. The reference program is written for one: setup_inputs(seed, part) draws one part's arguments, and reference() takes and returns one part's arrays. A program takes and returns all parts, laid end to end along the dimension named above; an argument that names none is the same for every part. Nothing has to cross between parts.
Inputs may be any that keep to these rules, and one draw needn't show every extreme that they name: `token_valid`: the ones come first.
All inputs are finite; a program needn't handle non-finite values.
Results may differ from the reference program's by a relative error of at most 0.014.
Values may be sent and summed in bfloat16 or wider, within the bound.
A program may use at most 64 MiB of HBM per device.

```python
import jax
import jax.numpy as jnp
from jax import lax

CPAIR = 128
ALIGN_CHANNELS = 64
COPM = 32
CHID = 512
TOKEN_COUNT = 256
ALIGN_ROWS = 128


def draw_alignment_mask(key, part):
    key_cover, key_vacant, key_keep = jax.random.split(jax.random.fold_in(key, 101), 3)
    coverage = jax.random.randint(key_cover, (TOKEN_COUNT,), ALIGN_ROWS // 2, ALIGN_ROWS + 1)
    vacant = jax.random.randint(key_vacant, (TOKEN_COUNT,), 0, 64)
    coverage = jnp.where(vacant == 0, 0, coverage)
    retained = jax.random.randint(key_keep, (ALIGN_ROWS, TOKEN_COUNT), 0, 8)
    seq_rows = jnp.arange(ALIGN_ROWS)[:, None]
    return ((seq_rows < coverage[None, :]) & (retained > 0)).astype(jnp.int32)


def draw_token_valid(key, part):
    length_key = jax.random.fold_in(key, 202)
    filled = jax.random.randint(length_key, (), TOKEN_COUNT - TOKEN_COUNT // 8, TOKEN_COUNT + 1)
    return (jnp.arange(TOKEN_COUNT) < filled).astype(jnp.int32)


def shard_levels(own_key, shape, cuts, low, largest):
    factor_of, own = 1.0, jax.random.fold_in(own_key, 6)
    for axis_at, shards_of in cuts:
        heights = jnp.exp(jax.random.uniform(jax.random.fold_in(own, axis_at), (shards_of,), jnp.float32, low / len(cuts), largest / len(cuts)))
        factor_of = factor_of * jnp.repeat(heights, shape[axis_at] // shards_of).reshape([-1 if axis == axis_at else 1 for axis in range(len(shape))])
    return factor_of


def bell_draw(stream_key, shape, deviation, reach, cuts=(), held_as=jnp.bfloat16):
    values = deviation * jax.random.normal(stream_key, shape, jnp.float32)
    if cuts:
        values = values * shard_levels(stream_key, shape, cuts, -0.22, 0.18)
    return jnp.clip(values, -reach, reach).astype(held_as)


def setup_inputs(seed: int = 0, part: int = 0) -> dict:
    splits = jax.random.split(jax.random.key(seed), 12)
    part_splits = jax.random.split(jax.random.fold_in(splits[11], part), 12)
    pair_input = bell_draw(part_splits[0], (TOKEN_COUNT, TOKEN_COUNT, CPAIR), 1.0, 6.0, ((0, 4), (1, 4)))
    alignment_features = bell_draw(part_splits[1], (ALIGN_ROWS, TOKEN_COUNT, ALIGN_CHANNELS), 1.0, 6.0, ((0, 4), (1, 4)))
    alignment_mask = draw_alignment_mask(jax.random.fold_in(jax.random.fold_in(splits[11], part), 71), part)
    token_valid = draw_token_valid(jax.random.fold_in(jax.random.fold_in(splits[11], part), 71), part)
    left_weight = bell_draw(splits[4], (ALIGN_CHANNELS, COPM), ALIGN_CHANNELS ** -0.5, 0.75)
    right_weight = bell_draw(splits[5], (ALIGN_CHANNELS, COPM), ALIGN_CHANNELS ** -0.5, 0.75)
    output_weight = bell_draw(splits[6], (COPM * COPM, CPAIR), 0.3, 1.75)
    gate_weight = bell_draw(splits[7], (CPAIR, CHID), CPAIR ** -0.5, 0.5)
    up_weight = bell_draw(splits[8], (CPAIR, CHID), CPAIR ** -0.5, 0.5)
    down_weight = bell_draw(splits[9], (CHID, CPAIR), CHID ** -0.5, 0.25)
    kernel_weight = bell_draw(splits[10], (3, 3, CPAIR, CPAIR), (9 * CPAIR) ** -0.5, 0.1875)
    return {"pair_input": pair_input, "alignment_features": alignment_features, "alignment_mask": alignment_mask, "token_valid": token_valid, "left_weight": left_weight, "right_weight": right_weight, "output_weight": output_weight, "gate_weight": gate_weight, "up_weight": up_weight, "down_weight": down_weight, "kernel_weight": kernel_weight}


epsilon = 1e-05
strip_rows = 16
slab_rows = 4096

def transition(pair_rows, gate_weight, up_weight, down_weight):
    values = pair_rows.astype(jnp.float32)
    centre = lax.optimization_barrier(jnp.mean(values, axis=-1, keepdims=True))
    spread = lax.optimization_barrier(jnp.mean(jnp.square(values - centre), axis=-1, keepdims=True))
    normed = ((values - centre) * lax.rsqrt(spread + epsilon)).astype(jnp.bfloat16)
    gate_act = jnp.dot(normed, gate_weight, preferred_element_type=jnp.float32)
    up_act = jnp.dot(normed, up_weight, preferred_element_type=jnp.float32)
    hidden = (jax.nn.silu(gate_act) * up_act).astype(jnp.bfloat16)
    return (values + jnp.dot(hidden, down_weight, preferred_element_type=jnp.float32)).astype(jnp.bfloat16)

def reference(pair_input, alignment_features, alignment_mask, token_valid, left_weight, right_weight, output_weight, gate_weight, up_weight, down_weight, kernel_weight):
    real_mask = alignment_mask.astype(jnp.float32)
    alignment_real = alignment_features.astype(jnp.float32)
    left_projected = (jnp.einsum('vdi,ie->vde', alignment_real, left_weight.astype(jnp.float32)) * real_mask[:, :, None]).astype(jnp.bfloat16)
    right_projected = (jnp.einsum('vdi,ie->vde', alignment_real, right_weight.astype(jnp.float32)) * real_mask[:, :, None]).astype(jnp.bfloat16)
    counts = jnp.dot(real_mask.T, real_mask, precision=lax.Precision.HIGHEST, preferred_element_type=jnp.float32)
    right_flat = right_projected.reshape(ALIGN_ROWS, TOKEN_COUNT * COPM)

    def outer_rows(first_row):
        left_part = lax.dynamic_slice_in_dim(left_projected, first_row, strip_rows, 1).reshape(ALIGN_ROWS, strip_rows * COPM)
        products = jnp.dot(left_part.T, right_flat, preferred_element_type=jnp.float32)
        products = products.reshape(strip_rows, COPM, TOKEN_COUNT, COPM).transpose(0, 2, 1, 3)
        products = products.reshape(strip_rows * TOKEN_COUNT, COPM * COPM).astype(jnp.bfloat16)
        update = jnp.dot(products, output_weight, preferred_element_type=jnp.float32).reshape(strip_rows, TOKEN_COUNT, CPAIR)
        pair_count = lax.dynamic_slice_in_dim(counts, first_row, strip_rows, 0)
        update = update / jnp.maximum(pair_count, 1.0)[:, :, None]
        base_pair = lax.dynamic_slice_in_dim(pair_input, first_row, strip_rows, 0).astype(jnp.float32)
        return (base_pair + update).astype(jnp.bfloat16)
    starts = jnp.arange(TOKEN_COUNT // strip_rows, dtype=jnp.int32) * strip_rows
    pair_one = lax.map(outer_rows, starts).reshape(TOKEN_COUNT, TOKEN_COUNT, CPAIR)

    def one_slab(pair_slab):
        return transition(pair_slab, gate_weight, up_weight, down_weight)
    pair_slabs = pair_one.reshape(TOKEN_COUNT * TOKEN_COUNT // slab_rows, slab_rows, CPAIR)
    pair_two = lax.map(one_slab, pair_slabs).reshape(TOKEN_COUNT, TOKEN_COUNT, CPAIR)
    pair_mirror = jnp.swapaxes(pair_two, 0, 1)
    pad_real = token_valid.astype(jnp.float32)
    symmetric = (pair_two.astype(jnp.float32) + pair_mirror.astype(jnp.float32)) * 0.5
    masked = (symmetric * pad_real[:, None, None] * pad_real[None, :, None]).astype(jnp.bfloat16)
    padded = jnp.pad(masked, ((1, 1), (1, 1), (0, 0)))

    def conv_rows(first_row):
        window = lax.dynamic_slice_in_dim(padded, first_row, strip_rows + 2, 0)
        summed = jnp.zeros((strip_rows * TOKEN_COUNT, CPAIR), jnp.float32)
        for shift_row in range(3):
            for shift_col in range(3):
                shifted = window[shift_row:shift_row + strip_rows, shift_col:shift_col + TOKEN_COUNT].reshape(strip_rows * TOKEN_COUNT, CPAIR)
                summed = summed + jnp.dot(shifted, kernel_weight[shift_row, shift_col], preferred_element_type=jnp.float32)
        centre = lax.dynamic_slice_in_dim(symmetric, first_row, strip_rows, 0).reshape(strip_rows * TOKEN_COUNT, CPAIR)
        return (centre + summed).astype(jnp.bfloat16).reshape(strip_rows, TOKEN_COUNT, CPAIR)
    return lax.map(conv_rows, starts).reshape(TOKEN_COUNT, TOKEN_COUNT, CPAIR)
```

```python
import functools

import jax
import jax.numpy as jnp
from jax import lax
from jax.experimental import pallas as pl
from jax.experimental.pallas import tpu as pltpu
from jax.sharding import PartitionSpec as P

epsilon = 1e-05
F32, BF16 = jnp.float32, jnp.bfloat16
MESH = pl.DeviceIdType.MESH
AROUND = [(a, b) for a in (-1, 0, 1) for b in (-1, 0, 1) if (a, b) != (0, 0)]


def dot(a, b):
    return jnp.dot(a, b, preferred_element_type=F32)


def block_kernel(
    sizes,
    feat_ref,
    mask_ref,
    valid_ref,
    wl_ref,
    wr_ref,
    *rest,
):
    far, (out_ref, *rest) = rest[:6], rest[6:]
    near, (w_sem, *rest) = rest[:6], rest[6:]
    pair_ref, wo_ref, wg_ref, wu_ref, wd_ref, wk_ref = near
    (
    proj,
    vrows,
    lsend,
    lg,
    rg,
    rt,
    rq,
    lcat,
    wof,
    w4,
    zs,
    rexp,
    ones,
    two,
    mirror,
    mf,
    sym,
    wide,
    colf,
    hsend,
    hrecv,
    l1_send,
    l1_recv,
    x_send,
    l2_send,
    l2_recv,
    r_send,
    r_recv,
    m_send,
    m_recv,
    relay,
    rl_send,
    rl_recv,
    h_send,
    h_recv,
    ) = rest
    rn, cn, chans, fold, rd, cd, ch, sl, tl, pw, cr = sizes
    row = lax.axis_index("row")
    col = lax.axis_index("col") * chans + lax.axis_index("chan")
    per = 128 // pw
    lgroups, rgroups = rd // per, cd // per
    cuts = min(4, rgroups)
    depth = rn * sl
    steps = rd // cr
    cgroups = cr // per

    def at(r, c):
        return {"row": r, "col": c // chans, "chan": c % chans}

    def remote(src, dst, ssem, rsem, r, c):
        return pltpu.make_async_remote_copy(
            src_ref=src, dst_ref=dst, send_sem=ssem, recv_sem=rsem,
            device_id=at(r, c), device_id_type=MESH,
        )

    order = (1, 0, 2, 3, 4, 5)
    loads = [pltpu.make_async_copy(far[n], near[n], w_sem.at[n]) for n in range(6)]
    for n in order:
        loads[n].start()
    hrecv[...] = jnp.zeros_like(hrecv)
    for i in (0, rd + 1):
        wide[i] = jnp.zeros((cd, 3 * ch), BF16)
    barrier = pltpu.get_barrier_semaphore()

    def greet(n, carry):
        pl.semaphore_signal(barrier, inc=1, device_id=at(n // cn, n % cn), device_id_type=MESH)
        return carry

    lax.fori_loop(0, rn * cn, greet, 0)

    spread = (
        lax.broadcasted_iota(jnp.int32, (pw, 128), 1) % pw
        == lax.broadcasted_iota(jnp.int32, (pw, 128), 0)
    ).astype(F32).astype(BF16)
    mask = mask_ref[...].astype(F32).astype(BF16)
    spots = tl // per
    token_of = (
        lax.broadcasted_iota(jnp.int32, (tl, spots * 128), 1) // pw
        == lax.broadcasted_iota(jnp.int32, (tl, spots * 128), 0)
    ).astype(F32).astype(BF16)
    wide_mask = dot(mask, token_of)
    feats = feat_ref[...].reshape(sl * tl, feat_ref.shape[2])
    lane_of = lax.broadcasted_iota(jnp.int32, (sl, 128), 1) // pw

    def project(n, w_ref):
        tiled = lax.dot_general(
            w_ref[...], spread, (((0,), (0,)), ((), ())), preferred_element_type=F32
        ).astype(BF16)
        proj[n] = dot(feats, tiled)
        parts = []
        for g in range(spots):
            got = proj[n, pl.ds(g * per, sl, stride=tl), :]
            for t in range(1, per):
                other = proj[n, pl.ds(g * per + t, sl, stride=tl), :]
                got = jnp.where(lane_of == t, other, got)
            parts.append((got * wide_mask[:, g * 128 : (g + 1) * 128]).astype(BF16))
        return parts

    left = project(0, wl_ref)
    for k in range(fold):
        for g in range(lgroups):
            lsend[k, 1 + g] = left[k * lgroups + g]
        lsend[k, 0] = jnp.zeros((sl, 128), BF16)
        lsend[k, 0, :, 0:rd] = mask[:, k * rd : (k + 1) * rd]
    pl.semaphore_wait(barrier, rn * cn)

    def span(n):
        if isinstance(n, int) and n == 0:
            return pl.ds(0, cgroups + 1)
        return pl.ds(1 + n * cgroups, cgroups)

    core, chip = col % chans, col // chans
    held = rn // chans
    home = row // fold // chans
    is_home = chip == home

    def l1_target(k):
        to_row, to_col = col * fold + k, chip * chans + row % chans
        return to_row, to_col, jnp.logical_and(to_row == row, to_col == col)

    def send_left(n):
        for k in range(fold):
            to_row, to_col, mine = l1_target(k)
            slot = row // chans
            src, dst = lsend.at[k, span(n)], lg.at[row, span(n)]

            @pl.when(mine)
            def _():
                pltpu.make_async_copy(src, dst, l1_recv.at[slot, n]).start()

            @pl.when(jnp.logical_not(mine))
            def _():
                remote(src, dst, l1_send.at[k, n], l1_recv.at[slot, n], to_row, to_col).start()

    chips = cn // chans

    def spread_left(i, at_home):
        m = (row // chans + i) % held
        for n in range(steps):
            piece = lg.at[m * chans + core, span(n)]
            pltpu.make_async_copy(piece, piece, l1_recv.at[m, n]).wait()
            if at_home:
                for d in range(1, chips):
                    remote(
                        piece, piece, x_send.at[m, d - 1, n], l1_recv.at[m, n],
                        row, (chip + d) % chips * chans + core,
                    ).start()
            for e in range(1, chans):
                remote(
                    piece, piece, l2_send.at[m, e - 1, n], l2_recv.at[m, e - 1, n],
                    row, chip * chans + (core + e) % chans,
                ).start()

    def take_left(n):
        for m in range(held):
            for e in range(1, chans):
                piece = lg.at[m * chans + (core + chans - e) % chans, span(n)]
                pltpu.make_async_copy(piece, piece, l2_recv.at[m, e - 1, n]).wait()

    for n in range(steps):
        send_left(n)

    right = project(1, wr_ref)
    for g in range(rgroups):
        rg[row, 1 + g] = right[g]
    rg[row, 0] = jnp.zeros((sl, 128), BF16)
    rg[row, 0, :, 0:tl] = mask

    def chain(t):
        low, high = jnp.maximum(row - t, 0), jnp.minimum(row + t, rn - 1)
        ups = jnp.logical_and(row - t >= 0, row + 1 < rn)
        downs = jnp.logical_and(row + t < rn, row >= 1)
        return (ups, low, row + 1), (downs, high, row - 1)

    quarter = rgroups // cuts
    pieces = [
        pl.ds(1 + e * quarter, quarter) if e else pl.ds(0, 1 + quarter) for e in range(cuts)
    ]

    upward = chip < chips // 2

    def pass_on(urgent):
        for way, (go, slot, to_row) in enumerate(chain(0)):

            @pl.when(jnp.logical_and(go, upward == (urgent == (way == 0))))
            def _():
                for e, piece in enumerate(pieces):
                    part_of = rg.at[slot, piece]
                    remote(
                        part_of, part_of, r_send.at[way, 0, e], r_recv.at[slot, e], to_row, col
                    ).start()

    pass_on(True)
    pass_on(False)

    tokens = valid_ref.shape[1]
    valid = valid_ref[...].astype(F32)

    def as_rows(first, count):
        hit = lax.broadcasted_iota(jnp.int32, (count, tokens), 1) == first + (
            lax.broadcasted_iota(jnp.int32, (count, tokens), 0)
        )
        chosen = jnp.where(hit, jnp.broadcast_to(valid, (count, tokens)), 0.0).astype(BF16)
        return dot(chosen, jnp.ones((tokens, ch), BF16))

    vrows[0:rd] = as_rows(row * rd, rd)
    valid_cols = as_rows(col * cd, cd)

    loads[1].wait()
    wof[...] = wo_ref[...].astype(F32)
    w4[...] = jnp.zeros_like(w4)
    for q in range(pw):
        part = wof[pl.ds(q, pw, stride=pw), :].astype(BF16)
        for i in range(per):
            w4[q * 128 + i * pw : q * 128 + (i + 1) * pw, i * ch : (i + 1) * ch] = part

    def hop(t, way):
        there_is, slot = (
            (row - t - 1 >= 0, jnp.maximum(row - t - 1, 0)),
            (row + t + 1 < rn, jnp.minimum(row + t + 1, rn - 1)),
        )[way]
        for e, piece in enumerate(pieces):

            @pl.when(there_is)
            def _():
                part_of = rg.at[slot, piece]
                pltpu.make_async_copy(part_of, part_of, r_recv.at[slot, e]).wait()

            if t + 1 < rn - 1:
                go, _slot, to_row = chain(t + 1)[way]

                @pl.when(go)
                def _():
                    part_of = rg.at[slot, piece]
                    remote(
                        part_of, part_of, r_send.at[way, t + 1, e], r_recv.at[slot, e],
                        to_row, col,
                    ).start()

    def hops(first, last, urgent):

        @pl.when(upward if urgent else jnp.logical_not(upward))
        def _():
            for t in range(first, last):
                hop(t, 0)

        @pl.when(jnp.logical_not(upward) if urgent else upward)
        def _():
            for t in range(first, last):
                hop(t, 1)

    ends = jnp.logical_or(row == 0, row == rn - 1)

    @pl.when(is_home)
    def _():
        spread_left(0, True)

    @pl.when(jnp.logical_and(is_home, ends))
    def _():
        for i in range(1, held):
            spread_left(i, True)

    @pl.when(jnp.logical_and(jnp.logical_not(is_home), ends))
    def _():
        for i in range(held):
            spread_left(i, False)

    hops(0, 1, True)

    @pl.when(jnp.logical_and(is_home, jnp.logical_not(ends)))
    def _():
        for i in range(1, held):
            spread_left(i, True)

    hops(1, rn - 1, True)

    @pl.when(jnp.logical_and(jnp.logical_not(is_home), jnp.logical_not(ends)))
    def _():
        for i in range(held):
            spread_left(i, False)

    hops(0, rn - 1, False)

    for g in range(rgroups):
        slab = rg[:, 1 + g].astype(F32).reshape(depth, 128)
        rt[g * 128 : (g + 1) * 128, :] = slab.T
    for q in range(pw):
        rq[q * cd : (q + 1) * cd, :] = rt[pl.ds(q, cd, stride=pw), :].astype(BF16)

    take_left(0)
    left_mask = lg[:, 0].astype(F32).reshape(depth, 128)
    right_mask = rg[:, 0].astype(F32).reshape(depth, 128)
    counts = dot(right_mask.T.astype(BF16), left_mask.astype(BF16))
    inverse = 1.0 / jnp.maximum(counts, 1.0)
    for i in range(rd):
        rexp[i] = jnp.broadcast_to(inverse[0:cd, i : i + 1], (cd, ch))

    for n in (0, 2, 3, 4, 5):
        loads[n].wait()

    qstep = min(8, pw)

    part = cr // 2

    def to_mirror(step, k, p):
        begin = step * cr + p * part
        src = two.at[pl.ds(begin, part), pl.ds(k * rd, rd)]
        dst = mirror.at[pl.ds((row % fold) * rd + begin, part)]
        return src, dst

    def send_mirror(step, k, p):
        to_row, to_col = col * fold + k, row // fold
        mine = jnp.logical_and(to_row == row, to_col == col)
        across = to_col // chans != chip
        at_end = jnp.logical_or(to_row == 0, to_row == rn - 1)
        turned = jnp.logical_and(across, at_end)
        src, dst = to_mirror(step, k, p)
        rsem = m_recv.at[row % fold, step, p]
        ssem = m_send.at[k, step, p]

        @pl.when(mine)
        def _():
            pltpu.make_async_copy(src, dst, rsem).start()

        @pl.when(turned)
        def _():
            slot = jnp.where(to_row == 0, 0, 1)
            remote(
                src, relay.at[slot, step, p], ssem, rl_recv.at[slot, step, p], row, to_col
            ).start()

        @pl.when(jnp.logical_not(jnp.logical_or(mine, turned)))
        def _():
            remote(src, dst, ssem, rsem, to_row, to_col).start()

    def relayed(slot):
        to_row = (0, rn - 1)[slot]
        active = jnp.logical_and(col == row // fold, to_row // fold // chans != chip)
        return active, to_row

    def forward(step):
        for slot in range(2):
            active, to_row = relayed(slot)

            @pl.when(active)
            def _():
                for p in (1, 0):
                    piece = relay.at[slot, step, p]
                    pltpu.make_async_copy(piece, piece, rl_recv.at[slot, step, p]).wait()
                    begin = (row % fold) * rd + step * cr + p * part
                    remote(
                        piece, mirror.at[pl.ds(begin, part)], rl_send.at[slot, step, p],
                        m_recv.at[row % fold, step, p], to_row, col,
                    ).start()

    def one_step(step, carry):

        @pl.when(step > 0)
        def _():
            take_left(step)

        @pl.when(2 * step < steps)
        def _():
            forward(2 * step)

        for g in range(cgroups):
            slab = lg[:, 1 + step * cgroups + g].astype(F32).reshape(depth, 128)
            lcat[0, :, g * 128 : (g + 1) * 128] = slab.astype(BF16)
        lpart = lcat[0]
        for q0 in range(0, pw, qstep):
            z = dot(rq[q0 * cd : (q0 + qstep) * cd, :], lpart).astype(BF16)
            for q in range(qstep):
                for g in range(cgroups):
                    zs[g * cd : (g + 1) * cd, (q0 + q) * 128 : (q0 + q + 1) * 128] = z[
                        q * cd : (q + 1) * cd, g * 128 : (g + 1) * 128
                    ]
        update = dot(zs[...], w4[...])
        for g in range(cgroups):
            for i in range(per):
                at_row = step * cr + g * per + i
                add = update[g * cd : (g + 1) * cd, i * ch : (i + 1) * ch] * rexp[at_row]
                ones[g * per + i] = (pair_ref[at_row].astype(F32) + add).astype(BF16)
        for p in (1, 0):
            values = ones[p * part : (p + 1) * part].reshape(part * cd, ch).astype(F32)
            centre = jnp.mean(values, axis=-1, keepdims=True)
            shifted = values - centre
            var = jnp.mean(jnp.square(shifted), axis=-1, keepdims=True)
            normed = (shifted * lax.rsqrt(var + epsilon)).astype(BF16)
            gate = dot(normed, wg_ref[...])
            up = dot(normed, wu_ref[...])
            hidden = (gate / (1.0 + jnp.exp(-gate)) * up).astype(BF16)
            result = (values + dot(hidden, wd_ref[...])).astype(BF16)
            two[pl.ds(step * cr + p * part, part)] = result.reshape(part, cd, ch)
            for k in range(fold):
                send_mirror(step, k, p)
            if p == 1:

                @pl.when(2 * step + 1 < steps)
                def _():
                    forward(2 * step + 1)

        return carry

    lax.fori_loop(0, steps, one_step, 0)

    stripes = cd // cr
    strip = min(32, rd)
    place = lax.broadcasted_iota(jnp.int32, (cr, ch), 0)

    def take_mirror(q):
        begin = q * cr
        k, step = begin // rd, begin % rd // cr
        for p in (1, 0):
            piece = mirror.at[pl.ds(begin + p * part, part)]
            pltpu.make_async_copy(piece, piece, m_recv.at[k, step, p]).wait()
        mf[begin * rd : (begin + cr) * rd, :] = (
            mirror[begin : begin + cr].astype(F32).reshape(cr * rd, ch)
        )
        some_cols = valid_cols[begin : begin + cr]

        def one_row(i, carry):
            other = mf[pl.ds(begin * rd + i, cr, stride=rd), :]
            half_sum = (two[i, begin : begin + cr].astype(F32) + other) * 0.5
            sym[i, begin : begin + cr] = half_sum
            masked = half_sum * some_cols * vrows[pl.ds(i, 1), :]
            wide[i + 1, begin : begin + cr, ch : 2 * ch] = masked.astype(BF16)
            before = colf[1, pl.ds(i, 1), :] if q else 0.0
            wide[i + 1, begin : begin + cr, 0:ch] = jnp.where(
                place == 0, before, pltpu.roll(masked, 1, 0)
            ).astype(BF16)
            if q:
                earlier = wide[i + 1, begin - cr : begin, ch : 2 * ch].astype(F32)
                wide[i + 1, begin - cr : begin, 2 * ch : 3 * ch] = jnp.where(
                    place == cr - 1, masked[0:1], pltpu.roll(earlier, cr - 1, 0)
                ).astype(BF16)
            else:
                colf[0, pl.ds(i, 1), :] = masked[0:1]
            if q == stripes - 1:
                wide[i + 1, begin : begin + cr, 2 * ch : 3 * ch] = jnp.where(
                    place == cr - 1, 0.0, pltpu.roll(masked, cr - 1, 0)
                ).astype(BF16)
            colf[1, pl.ds(i, 1), :] = masked[cr - 1 : cr]
            return carry

        lax.fori_loop(0, rd, one_row, 0, unroll=4)

    def conv(q):
        begin = q * cr
        for first in range(0, rd, strip):
            total = sym[first : first + strip, begin : begin + cr].reshape(strip * cr, ch)
            for a in range(3):
                window = wide[first + a : first + a + strip, begin : begin + cr]
                total = total + dot(window.reshape(strip * cr, 3 * ch), wk_ref[a])
            total = total.reshape(strip, cr, ch)
            out_ref[first : first + strip, begin : begin + cr] = total.astype(BF16)
            if q in (0, stripes - 1):
                sym[first : first + strip, begin : begin + cr] = total
            else:
                if first == 0:
                    sym[0, begin : begin + cr] = total[0]
                if first + strip == rd:
                    sym[rd - 1, begin : begin + cr] = total[strip - 1]

    for q in range(stripes):
        take_mirror(q)
        if 0 < q < stripes - 1:
            conv(q - 1)

    for n, (a, b) in enumerate(AROUND):
        if b == 0:
            hsend[n, 0:cd] = wide[1 if a < 0 else rd, :, ch : 2 * ch]
        elif a == 0:
            hsend[n, 0:rd] = colf[0 if b < 0 else 1].astype(BF16)
        else:
            corner = colf[0 if b < 0 else 1, 0:1] if a < 0 else colf[0 if b < 0 else 1, rd - 1 : rd]
            hsend[n, 0:16] = jnp.broadcast_to(corner, (16, ch)).astype(BF16)

    def there(a, b):
        r, c = row + a, col + b
        return jnp.logical_and(
            jnp.logical_and(r >= 0, r < rn), jnp.logical_and(c >= 0, c < cn)
        )

    def lines(a, b):
        return cd if b == 0 else (rd if a == 0 else 16)

    for n, (a, b) in enumerate(AROUND):

        @pl.when(there(a, b))
        def _():
            size = lines(a, b)
            remote(
                hsend.at[n, pl.ds(0, size)], hrecv.at[n, pl.ds(0, size)], h_send.at[n],
                h_recv.at[n], row + a, col + b,
            ).start()

    for q in range(max(stripes - 2, 0), stripes):
        conv(q)

    for n, (a, b) in enumerate(AROUND):

        @pl.when(there(-a, -b))
        def _():
            piece = hrecv.at[n, pl.ds(0, lines(a, b))]
            pltpu.make_async_copy(piece, piece, h_recv.at[n]).wait()

    slot_of = {direction: n for n, direction in enumerate(AROUND)}
    along = lax.broadcasted_iota(jnp.int32, (cd, ch), 0)
    down = lax.broadcasted_iota(jnp.int32, (rd, ch), 0)

    def edge_row(a, i):
        line = hrecv[slot_of[(a, 0)], 0:cd]
        centre = line.astype(F32)
        before = hrecv[slot_of[(a, 1)], 0:16].astype(F32)[0:1]
        after = hrecv[slot_of[(a, -1)], 0:16].astype(F32)[0:1]
        lefts = jnp.where(along == 0, before, pltpu.roll(centre, 1, 0)).astype(BF16)
        rights = jnp.where(along == cd - 1, after, pltpu.roll(centre, cd - 1, 0)).astype(BF16)
        w = 0 if a > 0 else 2
        sym[i] = sym[i] + (
            dot(lefts, wk_ref[w, 0:ch])
            + dot(line, wk_ref[w, ch : 2 * ch])
            + dot(rights, wk_ref[w, 2 * ch : 3 * ch])
        )

    def edge_col(b):
        line = hrecv[slot_of[(0, b)], 0:rd]
        centre = line.astype(F32)
        above = jnp.where(down == 0, 0.0, pltpu.roll(centre, 1, 0)).astype(BF16)
        below = jnp.where(down == rd - 1, 0.0, pltpu.roll(centre, rd - 1, 0)).astype(BF16)
        lo = 0 if b > 0 else 2 * ch
        return (
            dot(above, wk_ref[0, lo : lo + ch])
            + dot(line, wk_ref[1, lo : lo + ch])
            + dot(below, wk_ref[2, lo : lo + ch])
        )

    edge_row(1, 0)
    edge_row(-1, rd - 1)
    colf[0] = edge_col(1)
    colf[1] = edge_col(-1)
    for i in (0, rd - 1):
        out_ref[i] = sym[i].astype(BF16)

    def patch_row(i, carry):
        first = sym[i, 0:16]
        if cd == 16:
            first = first + jnp.where(place16 == 15, colf[1, pl.ds(i, 1), :], 0.0)
        out_ref[i, 0:16] = (
            first + jnp.where(place16 == 0, colf[0, pl.ds(i, 1), :], 0.0)
        ).astype(BF16)
        if cd > 16:
            out_ref[i, cd - 16 : cd] = (
                sym[i, cd - 16 : cd] + jnp.where(place16 == 15, colf[1, pl.ds(i, 1), :], 0.0)
            ).astype(BF16)
        return carry

    place16 = lax.broadcasted_iota(jnp.int32, (16, ch), 0)
    lax.fori_loop(0, rd, patch_row, 0, unroll=4)

    for k in range(fold):
        @pl.when(jnp.logical_not(l1_target(k)[2]))
        def _():
            for n in range(steps):
                piece = lsend.at[k, span(n)]
                pltpu.make_async_copy(piece, piece, l1_send.at[k, n]).wait()

        to_row, to_col = col * fold + k, row // fold

        @pl.when(jnp.logical_not(jnp.logical_and(to_row == row, to_col == col)))
        def _():
            for step in range(steps):
                for p in (0, 1):
                    src, _dst = to_mirror(step, k, p)
                    pltpu.make_async_copy(src, src, m_send.at[k, step, p]).wait()

    for slot in range(2):

        @pl.when(relayed(slot)[0])
        def _():
            for step in range(steps):
                for p in (0, 1):
                    piece = relay.at[slot, step, p]
                    pltpu.make_async_copy(piece, piece, rl_send.at[slot, step, p]).wait()

    for t in range(rn - 1):
        for way, (go, slot, _to_row) in enumerate(chain(t)):

            @pl.when(go)
            def _():
                for e, piece in enumerate(pieces):
                    part_of = rg.at[slot, piece]
                    pltpu.make_async_copy(part_of, part_of, r_send.at[way, t, e]).wait()

    for m in range(held):
        for n in range(steps):
            piece = lg.at[m * chans + core, span(n)]
            for e in range(1, chans):
                pltpu.make_async_copy(piece, piece, l2_send.at[m, e - 1, n]).wait()

    @pl.when(is_home)
    def _():
        for m in range(held):
            for n in range(steps):
                piece = lg.at[m * chans + core, span(n)]
                for d in range(1, chips):
                    pltpu.make_async_copy(piece, piece, x_send.at[m, d - 1, n]).wait()

    for n, (a, b) in enumerate(AROUND):

        @pl.when(there(a, b))
        def _():
            piece = hsend.at[n, pl.ds(0, lines(a, b))]
            pltpu.make_async_copy(piece, piece, h_send.at[n]).wait()


def on_device(
    mesh_shape,
    pair_input,
    alignment_features,
    alignment_mask,
    token_valid,
    left_weight,
    right_weight,
    output_weight,
    gate_weight,
    up_weight,
    down_weight,
    kernel_weight,
):
    rd, cd, ch = pair_input.shape
    sl, tl, aw = alignment_features.shape
    pw = left_weight.shape[1]
    hid = gate_weight.shape[1]
    rn, chans = mesh_shape["row"], mesh_shape["chan"]
    cn = mesh_shape["col"] * chans
    fold = rn // cn
    per = 128 // pw
    cr = min(16, rd)
    depth = rn * sl
    steps = rd // cr
    tall = max(rd, cd, 16)
    wk = kernel_weight.reshape(3, 3 * ch, ch)
    sizes = (rn, cn, chans, fold, rd, cd, ch, sl, tl, pw, cr)
    large = (pair_input, output_weight, gate_weight, up_weight, down_weight, wk)
    dma = pltpu.SemaphoreType.DMA
    vmem = pl.BlockSpec(memory_space=pltpu.VMEM)
    return pl.pallas_call(
        functools.partial(block_kernel, sizes),
        out_shape=jax.ShapeDtypeStruct((rd, cd, ch), BF16),
        in_specs=[vmem] * 5 + [pl.BlockSpec(memory_space=pl.ANY)] * 6,
        out_specs=vmem,
        scratch_shapes=[
            *[pltpu.VMEM(value.shape, value.dtype) for value in large],
            dma((6,)),
            pltpu.VMEM((2, sl * tl, 128), F32),
            pltpu.VMEM((tall, ch), F32),
            pltpu.VMEM((fold, rd // per + 1, sl, 128), BF16),
            pltpu.VMEM((rn, rd // per + 1, sl, 128), BF16),
            pltpu.VMEM((rn, cd // per + 1, sl, 128), BF16),
            pltpu.VMEM((cd * pw, depth), F32),
            pltpu.VMEM((pw * cd, depth), BF16),
            pltpu.VMEM((1, depth, cr * pw), BF16),
            pltpu.VMEM((pw * pw, ch), F32),
            pltpu.VMEM((pw * 128, per * ch), BF16),
            pltpu.VMEM((cr // per * cd, pw * 128), BF16),
            pltpu.VMEM((rd, cd, ch), F32),
            pltpu.VMEM((cr, cd, ch), BF16),
            pltpu.VMEM((rd, cd, ch), BF16),
            pltpu.VMEM((cd, rd, ch), BF16),
            pltpu.VMEM((cd * rd, ch), F32),
            pltpu.VMEM((rd, cd, ch), F32),
            pltpu.VMEM((rd + 2, cd, 3 * ch), BF16),
            pltpu.VMEM((2, rd, ch), F32),
            pltpu.VMEM((8, tall, ch), BF16),
            pltpu.VMEM((8, tall, ch), BF16),
            dma((fold, steps)),
            dma((rn // chans, steps)),
            dma((rn // chans, max(cn // chans - 1, 1), steps)),
            dma((rn // chans, max(chans - 1, 1), steps)),
            dma((rn // chans, max(chans - 1, 1), steps)),
            dma((2, rn - 1, min(4, cd // per))),
            dma((rn, min(4, cd // per))),
            dma((fold, steps, 2)),
            dma((fold, steps, 2)),
            pltpu.VMEM((2, steps, 2, cr // 2, rd, ch), BF16),
            dma((2, steps, 2)),
            dma((2, steps, 2)),
            dma((8,)),
            dma((8,)),
        ],
        compiler_params=pltpu.CompilerParams(
            collective_id=0, has_side_effects=True, vmem_limit_bytes=44 * 1024 * 1024
        ),
    )(
        *[
            pltpu.with_memory_space_constraint(value, pltpu.HBM)
            for value in (
                alignment_features,
                alignment_mask,
                token_valid.reshape(1, -1),
                left_weight.T,
                right_weight.T,
                *large,
            )
        ]
    )


def solution(mesh):
    placed = (
        P(("groups", "row"), ("col", "chan"), None),
        P("row", ("groups", "col", "chan"), None),
        P("row", ("groups", "col", "chan")),
        P("groups"),
        P(),
        P(),
        P(),
        P(),
        P(),
        P(),
        P(),
    )
    return jax.shard_map(
        functools.partial(on_device, dict(mesh.shape)),
        mesh=mesh,
        in_specs=placed,
        out_specs=P(("groups", "row"), ("col", "chan"), None),
        check_vma=False,
    )
```

```python
import functools

import jax
import jax.numpy as jnp
from jax import lax
from jax.experimental import pallas as pl
from jax.experimental.pallas import tpu as pltpu
from jax.sharding import PartitionSpec as P

epsilon = 1e-05
F32, BF16 = jnp.float32, jnp.bfloat16
MESH = pl.DeviceIdType.MESH
AROUND = [(a, b) for a in (-1, 0, 1) for b in (-1, 0, 1) if (a, b) != (0, 0)]


def dot(a, b):
    return jnp.dot(a, b, preferred_element_type=F32)


def block_kernel(sizes, *refs):
    far, (out_ref, *rest) = refs[:11], refs[11:]
    near, (w_sem, *rest) = rest[:11], rest[11:]
    feat_ref, mask_ref, valid_ref, wl_ref, wr_ref = near[:5]
    pair_ref, wo_ref, wg_ref, wu_ref, wd_ref, wk_ref = near[5:]
    (
    proj,
    vrows,
    lsend,
    lg,
    rg,
    rt,
    rq,
    lcat,
    wof,
    w2,
    zs,
    rexp,
    inv,
    ones,
    two,
    mirror,
    mf,
    sym,
    wide,
    colf,
    hsend,
    hrecv,
    result,
    l1_send,
    l1_recv,
    x_send,
    l2_send,
    l2_recv,
    r_send,
    r_recv,
    m_send,
    m_recv,
    relay,
    rl_send,
    rl_recv,
    h_send,
    h_recv,
    o_sem,
    ) = rest
    rn, cn, chans, fold, rd, cd, ch, sl, tl, pw, cr = sizes
    row = lax.axis_index("row")
    col = lax.axis_index("col") * chans + lax.axis_index("chan")
    per = 128 // pw
    lgroups, rgroups = rd // per, cd // per
    cuts = min(4, rgroups)
    depth = rn * sl
    steps = rd // cr
    cgroups = cr // per
    half = cd // 2
    seg = min(half, rd)
    subs = rd // seg

    def at(r, c):
        return {"row": r, "col": c // chans, "chan": c % chans}

    def remote(src, dst, ssem, rsem, r, c):
        return pltpu.make_async_remote_copy(
            src_ref=src, dst_ref=dst, send_sem=ssem, recv_sem=rsem,
            device_id=at(r, c), device_id_type=MESH,
        )

    loads = [pltpu.make_async_copy(far[n], near[n], w_sem.at[n]) for n in range(11)]
    for n in (0, 1, 3, 4, 2, 6, 5, 7, 8, 9, 10):
        loads[n].start()
    barrier = pltpu.get_barrier_semaphore()

    def greet(n, carry):
        pl.semaphore_signal(barrier, inc=1, device_id=at(n // cn, n % cn), device_id_type=MESH)
        return carry

    lax.fori_loop(0, rn * cn, greet, 0)
    hrecv[...] = jnp.zeros_like(hrecv)
    for i in (0, rd + 1):
        wide[i] = jnp.zeros((cd, 3 * ch), BF16)

    spread = (
        lax.broadcasted_iota(jnp.int32, (pw, 128), 1) % pw
        == lax.broadcasted_iota(jnp.int32, (pw, 128), 0)
    ).astype(F32).astype(BF16)
    for n in (0, 1, 3, 4):
        loads[n].wait()
    mask = mask_ref[...].astype(F32).astype(BF16)
    spots = tl // per
    token_of = (
        lax.broadcasted_iota(jnp.int32, (tl, spots * 128), 1) // pw
        == lax.broadcasted_iota(jnp.int32, (tl, spots * 128), 0)
    ).astype(F32).astype(BF16)
    wide_mask = dot(mask, token_of)
    feats = feat_ref[...].reshape(sl * tl, feat_ref.shape[2])
    lane_of = lax.broadcasted_iota(jnp.int32, (sl, 128), 1) // pw

    def project(n, w_ref):
        tiled = lax.dot_general(
            w_ref[...], spread, (((0,), (0,)), ((), ())), preferred_element_type=F32
        ).astype(BF16)
        proj[n] = dot(feats, tiled)
        parts = []
        for g in range(spots):
            got = proj[n, pl.ds(g * per, sl, stride=tl), :]
            for t in range(1, per):
                other = proj[n, pl.ds(g * per + t, sl, stride=tl), :]
                got = jnp.where(lane_of == t, other, got)
            parts.append((got * wide_mask[:, g * 128 : (g + 1) * 128]).astype(BF16))
        return parts

    left = project(0, wl_ref)
    for k in range(fold):
        for g in range(lgroups):
            lsend[k, 1 + g] = left[k * lgroups + g]
        lsend[k, 0] = jnp.zeros((sl, 128), BF16)
        lsend[k, 0, :, 0:rd] = mask[:, k * rd : (k + 1) * rd]
    def project_right():
        right = project(1, wr_ref)
        for g in range(rgroups):
            rg[row, 1 + g] = right[g]
        rg[row, 0] = jnp.zeros((sl, 128), BF16)
        rg[row, 0, :, 0:tl] = mask

    early = row < rn // 2

    @pl.when(early)
    def _():
        project_right()


    pl.semaphore_wait(barrier, rn * cn)

    def span(n):
        if isinstance(n, int) and n == 0:
            return pl.ds(0, cgroups + 1)
        return pl.ds(1 + n * cgroups, cgroups)

    core, chip = col % chans, col // chans
    held = rn // chans
    home = row // fold // chans
    is_home = chip == home

    def l1_target(k):
        to_row, to_col = col * fold + k, chip * chans + row % chans
        return to_row, to_col, jnp.logical_and(to_row == row, to_col == col)

    def send_left(n):
        for k in range(fold):
            to_row, to_col, mine = l1_target(k)
            slot = row // chans
            src, dst = lsend.at[k, span(n)], lg.at[row, span(n)]

            @pl.when(mine)
            def _():
                pltpu.make_async_copy(src, dst, l1_recv.at[slot, n]).start()

            @pl.when(jnp.logical_not(mine))
            def _():
                remote(src, dst, l1_send.at[k, n], l1_recv.at[slot, n], to_row, to_col).start()

    chips = cn // chans

    def spread_left(i, n, at_home):
        m = (row // chans + i) % held
        piece = lg.at[m * chans + core, span(n)]
        pltpu.make_async_copy(piece, piece, l1_recv.at[m, n]).wait()
        if at_home:
            for d in range(1, chips):
                remote(
                    piece, piece, x_send.at[m, d - 1, n], l1_recv.at[m, n],
                    row, (chip + d) % chips * chans + core,
                ).start()
        for e in range(1, chans):
            remote(
                piece, piece, l2_send.at[m, e - 1, n], l2_recv.at[m, e - 1, n],
                row, chip * chans + (core + e) % chans,
            ).start()

    def take_left(n):
        for m in range(held):
            for e in range(1, chans):
                piece = lg.at[m * chans + (core + chans - e) % chans, span(n)]
                pltpu.make_async_copy(piece, piece, l2_recv.at[m, e - 1, n]).wait()

    send_left(0)

    @pl.when(jnp.logical_not(early))
    def _():
        project_right()

    def chain(t):
        low, high = jnp.maximum(row - t, 0), jnp.minimum(row + t, rn - 1)
        ups = jnp.logical_and(row - t >= 0, row + 1 < rn)
        downs = jnp.logical_and(row + t < rn, row >= 1)
        return (ups, low, row + 1), (downs, high, row - 1)

    quarter = rgroups // cuts
    pieces = [
        pl.ds(1 + e * quarter, quarter) if e else pl.ds(0, 1 + quarter) for e in range(cuts)
    ]

    upward = chip < chips // 2

    def pass_on(urgent, later):
        for way, (go, slot, to_row) in enumerate(chain(0)):

            @pl.when(jnp.logical_and(go, upward == (urgent == (way == 0))))
            def _():
                for e in cut_range(later):
                    part_of = rg.at[slot, pieces[e]]
                    remote(
                        part_of, part_of, r_send.at[way, 0, e], r_recv.at[slot, e], to_row, col
                    ).start()

    def cut_range(later):
        return range(cuts // 2, cuts) if later else range(cuts // 2)

    pass_on(True, False)
    pass_on(False, False)
    for n in range(1, steps):
        send_left(n)

    loads[2].wait()
    tokens = valid_ref.shape[1]
    valid = valid_ref[...].astype(F32)

    def as_rows(first, count):
        hit = lax.broadcasted_iota(jnp.int32, (count, tokens), 1) == first + (
            lax.broadcasted_iota(jnp.int32, (count, tokens), 0)
        )
        chosen = jnp.where(hit, jnp.broadcast_to(valid, (count, tokens)), 0.0).astype(BF16)
        return dot(chosen, jnp.ones((tokens, ch), BF16))

    vrows[0:rd] = as_rows(row * rd, rd)
    valid_cols = as_rows(col * cd, cd)

    loads[6].wait()
    wof[...] = wo_ref[...].astype(F32)
    w2[...] = jnp.zeros_like(w2)
    for q in range(pw):
        values = wof[pl.ds(q, pw, stride=pw), :].astype(BF16)
        for i in range(2):
            begin = q // 2 * 128 + (q % 2 * 2 + i) * pw
            w2[begin : begin + pw, i * ch : (i + 1) * ch] = values

    def hop(t, way, later):
        there_is, slot = (
            (row - t - 1 >= 0, jnp.maximum(row - t - 1, 0)),
            (row + t + 1 < rn, jnp.minimum(row + t + 1, rn - 1)),
        )[way]
        for e in cut_range(later):
            piece = pieces[e]

            @pl.when(there_is)
            def _():
                part_of = rg.at[slot, piece]
                pltpu.make_async_copy(part_of, part_of, r_recv.at[slot, e]).wait()

            if t + 1 < rn - 1:
                go, _slot, to_row = chain(t + 1)[way]

                @pl.when(go)
                def _():
                    part_of = rg.at[slot, piece]
                    remote(
                        part_of, part_of, r_send.at[way, t + 1, e], r_recv.at[slot, e],
                        to_row, col,
                    ).start()

    def hops(first, last, urgent, later=False):

        @pl.when(upward if urgent else jnp.logical_not(upward))
        def _():
            for t in range(first, last):
                hop(t, 0, later)

        @pl.when(jnp.logical_not(upward) if urgent else upward)
        def _():
            for t in range(first, last):
                hop(t, 1, later)

    ends = jnp.logical_or(row == 0, row == rn - 1)
    inner = jnp.logical_not(ends)
    away = jnp.logical_not(is_home)

    @pl.when(is_home)
    def _():
        spread_left(0, 0, True)

    @pl.when(jnp.logical_and(is_home, ends))
    def _():
        for i in range(1, held):
            spread_left(i, 0, True)

    @pl.when(jnp.logical_and(away, ends))
    def _():
        for i in range(held):
            spread_left(i, 0, False)

    hops(0, 1, True)
    pass_on(True, True)

    @pl.when(ends)
    def _():
        pass_on(False, True)


    @pl.when(jnp.logical_and(is_home, inner))
    def _():
        for i in range(1, held):
            spread_left(i, 0, True)

    hops(1, rn - 1, True)

    @pl.when(jnp.logical_and(away, inner))
    def _():
        for i in range(held):
            spread_left(i, 0, False)

    @pl.when(is_home)
    def _():
        for n in range(1, steps):
            for i in range(held):
                spread_left(i, n, True)

    @pl.when(is_home)
    def _():
        hops(0, 1, True, True)

    hops(0, rn - 1, False)

    @pl.when(inner)
    def _():
        pass_on(False, True)

    take_left(0)
    left_mask = lg[:, 0].astype(F32).reshape(depth, 128)
    right_mask = rg[:, 0].astype(F32).reshape(depth, 128)
    counts = dot(right_mask.T.astype(BF16), left_mask.astype(BF16))
    inv[...] = 1.0 / jnp.maximum(counts, 1.0)

    def prepare(h):
        for g in range(h * rgroups // 2, (h + 1) * rgroups // 2):
            slab = rg[:, 1 + g].astype(F32).reshape(depth, 128)
            rt[g * 128 : (g + 1) * 128, :] = slab.T
        for q in range(pw):
            rq[h, q // 2 * half : (q // 2 + 1) * half, q % 2 * depth : (q % 2 + 1) * depth] = rt[
                pl.ds(h * half * pw + q, half, stride=pw), :
            ].astype(BF16)
        inverse = inv[h * half : (h + 1) * half]
        for i in range(rd):
            rexp[i, h * half : (h + 1) * half] = jnp.broadcast_to(
                inverse[:, i : i + 1], (half, ch)
            )

    prepare(0)

    for n in (5, 7, 8, 9, 10):
        loads[n].wait()

    lag = 0

    def segments(h):
        found = []
        for begin in range(h * half, (h + 1) * half, seg):
            found.append((begin, begin // rd, begin % rd))
        return found

    def send_mirror(h, step):
        for begin, k, off in segments(h):
            to_row, to_col = col * fold + k, row // fold
            mine = jnp.logical_and(to_row == row, to_col == col)
            across = to_col // chans != chip
            at_end = jnp.logical_or(to_row == 0, to_row == rn - 1)
            turned = jnp.logical_and(across, at_end)
            sub = off // seg
            src = two.at[pl.ds(step * cr, cr), pl.ds(begin, seg)]
            dst = mirror.at[pl.ds(row % fold * rd + step * cr, cr), pl.ds(off, seg)]
            rsem = m_recv.at[row % fold, step, sub]
            ssem = m_send.at[k, step, sub]

            @pl.when(mine)
            def _():
                pltpu.make_async_copy(src, dst, rsem).start()

            @pl.when(turned)
            def _():
                slot = jnp.where(to_row == 0, 0, 1)
                remote(
                    src, relay.at[slot, step, sub], ssem, rl_recv.at[slot, step, sub],
                    row, to_col,
                ).start()

            @pl.when(jnp.logical_not(jnp.logical_or(mine, turned)))
            def _():
                remote(src, dst, ssem, rsem, to_row, to_col).start()

    def relayed(slot):
        to_row = (0, rn - 1)[slot]
        active = jnp.logical_and(col == row // fold, to_row // fold // chans != chip)
        return active, to_row

    def forward(h, step):
        for slot in range(2):
            active, to_row = relayed(slot)
            for _begin, k, off in segments(h):
                if k == to_row % fold:
                    sub = off // seg

                    @pl.when(active)
                    def _():
                        piece = relay.at[slot, step, sub]
                        pltpu.make_async_copy(piece, piece, rl_recv.at[slot, step, sub]).wait()
                        remote(
                            piece,
                            mirror.at[pl.ds(row % fold * rd + step * cr, cr), pl.ds(off, seg)],
                            rl_send.at[slot, step, sub],
                            m_recv.at[row % fold, step, sub], to_row, col,
                        ).start()

    low_lanes = lax.broadcasted_iota(jnp.int32, (depth, 128), 1) < 64

    def serve(step):
        for t in range(rn - 1):

            @pl.when(step == min(t, steps - 1))
            def _():
                for way in (0, 1):
                    if t:
                        hop(t, way, True)
                    else:

                        @pl.when(jnp.logical_or(away, upward == (way == 1)))
                        def _():
                            hop(0, way, True)

        @pl.when(jnp.logical_and(away, step + 1 < steps))
        def _():
            for i in range(held):
                spread_left(i, step + 1, False)

        @pl.when(step > 0)
        def _():
            take_left(step)

    def one_step(h, step):
        lo = h * half
        if h == 0:
            serve(step)

        @pl.when(step >= lag)
        def _():
            forward(h, step - lag)

        if h and lag:

            @pl.when(step < lag)
            def _():
                forward(h - 1, steps - lag + step)

        for g in range(cgroups):
            slab = lg[:, 1 + step * cgroups + g].astype(F32).reshape(depth, 128)
            turned = pltpu.roll(slab, 64, 1)
            for i, (first, second) in enumerate(((slab, turned), (turned, slab))):
                at_lane = (g * 2 + i) * 128
                lcat[0:depth, at_lane : at_lane + 128] = jnp.where(low_lanes, first, 0.0).astype(BF16)
                lcat[depth : 2 * depth, at_lane : at_lane + 128] = jnp.where(
                    low_lanes, 0.0, second
                ).astype(BF16)
        for g in range(cgroups):
            z = dot(rq[h], lcat[:, g * 256 : (g + 1) * 256]).astype(BF16)
            for i in range(2):
                for q in range(pw // 2):
                    begin = (i * cgroups + g) * half
                    zs[begin : begin + half, q * 128 : (q + 1) * 128] = z[
                        q * half : (q + 1) * half, i * 128 : (i + 1) * 128
                    ]
        update = dot(zs[...], w2[...])
        for g in range(cgroups):
            for i in range(per):
                at_row = step * cr + g * per + i
                begin = (i // 2 * cgroups + g) * half
                add = update[begin : begin + half, i % 2 * ch : (i % 2 + 1) * ch]
                add = add * rexp[at_row, lo : lo + half]
                ones[g * per + i] = (pair_ref[at_row, lo : lo + half].astype(F32) + add).astype(BF16)
        values = ones[...].reshape(cr * half, ch).astype(F32)
        centre = jnp.mean(values, axis=-1, keepdims=True)
        shifted = values - centre
        var = jnp.mean(jnp.square(shifted), axis=-1, keepdims=True)
        normed = (shifted * lax.rsqrt(var + epsilon)).astype(BF16)
        gate = dot(normed, wg_ref[...])
        up = dot(normed, wu_ref[...])
        hidden = (gate / (1.0 + jnp.exp(-gate)) * up).astype(BF16)
        done = (values + dot(hidden, wd_ref[...])).astype(BF16)
        two[pl.ds(step * cr, cr), lo : lo + half] = done.reshape(cr, half, ch)
        send_mirror(h, step)

    def run(h):
        def body(step, carry):
            one_step(h, step)
            return carry

        lax.fori_loop(0, steps, body, 0)

    run(0)
    prepare(1)
    run(1)
    for step in range(steps - lag, steps):
        forward(1, step)

    stripes = cd // cr
    place = lax.broadcasted_iota(jnp.int32, (cr, ch), 0)

    def take_mirror(sub, q):
        begin = q * cr
        k, step = begin // rd, begin % rd // cr
        top = sub * seg
        piece = mirror.at[pl.ds(begin, cr), pl.ds(top, seg)]
        pltpu.make_async_copy(piece, piece, m_recv.at[k, step, sub]).wait()
        mf[0 : cr * seg] = (
            mirror[begin : begin + cr, top : top + seg].astype(F32).reshape(cr * seg, ch)
        )
        some_cols = valid_cols[begin : begin + cr]

        def one_row(i, carry):
            other = mf[pl.ds(i - top, cr, stride=seg), :]
            half_sum = (two[i, begin : begin + cr].astype(F32) + other) * 0.5
            sym[i, begin : begin + cr] = half_sum
            masked = half_sum * some_cols * vrows[pl.ds(i, 1), :]
            wide[i + 1, begin : begin + cr, ch : 2 * ch] = masked.astype(BF16)
            before = colf[1, pl.ds(i, 1), :] if q else 0.0
            wide[i + 1, begin : begin + cr, 0:ch] = jnp.where(
                place == 0, before, pltpu.roll(masked, 1, 0)
            ).astype(BF16)
            if q:
                earlier = wide[i + 1, begin - cr : begin, ch : 2 * ch].astype(F32)
                wide[i + 1, begin - cr : begin, 2 * ch : 3 * ch] = jnp.where(
                    place == cr - 1, masked[0:1], pltpu.roll(earlier, cr - 1, 0)
                ).astype(BF16)
            else:
                colf[0, pl.ds(i, 1), :] = masked[0:1]
            if q == stripes - 1:
                wide[i + 1, begin : begin + cr, 2 * ch : 3 * ch] = jnp.where(
                    place == cr - 1, 0.0, pltpu.roll(masked, cr - 1, 0)
                ).astype(BF16)
            colf[1, pl.ds(i, 1), :] = masked[cr - 1 : cr]
            return carry

        lax.fori_loop(top, top + seg, one_row, 0, unroll=4)

    strip = min(32, rd)

    def conv(q):
        begin = q * cr
        for first in range(0, rd, strip):
            total = sym[first : first + strip, begin : begin + cr].reshape(strip * cr, ch)
            for a in range(3):
                window = wide[first + a : first + a + strip, begin : begin + cr]
                total = total + dot(window.reshape(strip * cr, 3 * ch), wk_ref[a])
            total = total.reshape(strip, cr, ch)
            result[first : first + strip, begin : begin + cr] = total.astype(BF16)
            if q in (0, stripes - 1):
                sym[first : first + strip, begin : begin + cr] = total
            else:
                if first == 0:
                    sym[0, begin : begin + cr] = total[0]
                if first + strip == rd:
                    sym[rd - 1, begin : begin + cr] = total[strip - 1]
        if 0 < q < stripes - 1:
            middle(q).start()

    def middle(q):
        block = (pl.ds(1, rd - 2), pl.ds(q * cr, cr))
        return pltpu.make_async_copy(result.at[block], out_ref.at[block], o_sem.at[0, q])

    for sub in range(subs):
        for q in range(stripes):
            take_mirror(sub, q)
            if sub == subs - 1 and 0 < q < stripes - 1:
                conv(q - 1)

    for n, (a, b) in enumerate(AROUND):
        if b == 0:
            hsend[n, 0:cd] = wide[1 if a < 0 else rd, :, ch : 2 * ch]
        elif a == 0:
            hsend[n, 0:rd] = colf[0 if b < 0 else 1].astype(BF16)
        else:
            corner = colf[0 if b < 0 else 1, 0:1] if a < 0 else colf[0 if b < 0 else 1, rd - 1 : rd]
            hsend[n, 0:16] = jnp.broadcast_to(corner, (16, ch)).astype(BF16)

    def there(a, b):
        r, c = row + a, col + b
        return jnp.logical_and(
            jnp.logical_and(r >= 0, r < rn), jnp.logical_and(c >= 0, c < cn)
        )

    def lines(a, b):
        return cd if b == 0 else (rd if a == 0 else 16)

    for n, (a, b) in enumerate(AROUND):

        @pl.when(there(a, b))
        def _():
            size = lines(a, b)
            remote(
                hsend.at[n, pl.ds(0, size)], hrecv.at[n, pl.ds(0, size)], h_send.at[n],
                h_recv.at[n], row + a, col + b,
            ).start()

    for q in range(max(stripes - 2, 0), stripes):
        conv(q)

    for n, (a, b) in enumerate(AROUND):

        @pl.when(there(-a, -b))
        def _():
            piece = hrecv.at[n, pl.ds(0, lines(a, b))]
            pltpu.make_async_copy(piece, piece, h_recv.at[n]).wait()

    slot_of = {direction: n for n, direction in enumerate(AROUND)}
    along = lax.broadcasted_iota(jnp.int32, (cd, ch), 0)
    down = lax.broadcasted_iota(jnp.int32, (rd, ch), 0)

    def edge_row(a, i):
        line = hrecv[slot_of[(a, 0)], 0:cd]
        centre = line.astype(F32)
        before = hrecv[slot_of[(a, 1)], 0:16].astype(F32)[0:1]
        after = hrecv[slot_of[(a, -1)], 0:16].astype(F32)[0:1]
        lefts = jnp.where(along == 0, before, pltpu.roll(centre, 1, 0)).astype(BF16)
        rights = jnp.where(along == cd - 1, after, pltpu.roll(centre, cd - 1, 0)).astype(BF16)
        w = 0 if a > 0 else 2
        sym[i] = sym[i] + (
            dot(lefts, wk_ref[w, 0:ch])
            + dot(line, wk_ref[w, ch : 2 * ch])
            + dot(rights, wk_ref[w, 2 * ch : 3 * ch])
        )

    def edge_col(b):
        line = hrecv[slot_of[(0, b)], 0:rd]
        centre = line.astype(F32)
        above = jnp.where(down == 0, 0.0, pltpu.roll(centre, 1, 0)).astype(BF16)
        below = jnp.where(down == rd - 1, 0.0, pltpu.roll(centre, rd - 1, 0)).astype(BF16)
        lo = 0 if b > 0 else 2 * ch
        return (
            dot(above, wk_ref[0, lo : lo + ch])
            + dot(line, wk_ref[1, lo : lo + ch])
            + dot(below, wk_ref[2, lo : lo + ch])
        )

    edge_row(1, 0)
    edge_row(-1, rd - 1)
    colf[0] = edge_col(1)
    colf[1] = edge_col(-1)
    for i in (0, rd - 1):
        result[i] = sym[i].astype(BF16)

    def patch_row(i, carry):
        first = sym[i, 0:16]
        if cd == 16:
            first = first + jnp.where(place16 == 15, colf[1, pl.ds(i, 1), :], 0.0)
        result[i, 0:16] = (
            first + jnp.where(place16 == 0, colf[0, pl.ds(i, 1), :], 0.0)
        ).astype(BF16)
        if cd > 16:
            result[i, cd - 16 : cd] = (
                sym[i, cd - 16 : cd] + jnp.where(place16 == 15, colf[1, pl.ds(i, 1), :], 0.0)
            ).astype(BF16)
        return carry

    place16 = lax.broadcasted_iota(jnp.int32, (16, ch), 0)
    lax.fori_loop(0, rd, patch_row, 0, unroll=4)

    closing = []
    for n, i in enumerate((0, rd - 1)):
        closing.append(pltpu.make_async_copy(result.at[i], out_ref.at[i], o_sem.at[1, n]))
    for n, q in enumerate((0, stripes - 1)):
        block = (pl.ds(1, rd - 2), pl.ds(q * cr, cr))
        closing.append(
            pltpu.make_async_copy(result.at[block], out_ref.at[block], o_sem.at[2, n])
        )
    for copy in closing:
        copy.start()

    for k in range(fold):
        @pl.when(jnp.logical_not(l1_target(k)[2]))
        def _():
            for n in range(steps):
                piece = lsend.at[k, span(n)]
                pltpu.make_async_copy(piece, piece, l1_send.at[k, n]).wait()

        to_row, to_col = col * fold + k, row // fold

        @pl.when(jnp.logical_not(jnp.logical_and(to_row == row, to_col == col)))
        def _():
            for step in range(steps):
                for sub in range(subs):
                    src = two.at[pl.ds(step * cr, cr), pl.ds(k * rd + sub * seg, seg)]
                    pltpu.make_async_copy(src, src, m_send.at[k, step, sub]).wait()

    for slot in range(2):

        @pl.when(relayed(slot)[0])
        def _():
            for step in range(steps):
                for sub in range(subs):
                    piece = relay.at[slot, step, sub]
                    pltpu.make_async_copy(piece, piece, rl_send.at[slot, step, sub]).wait()

    for t in range(rn - 1):
        for way, (go, slot, _to_row) in enumerate(chain(t)):

            @pl.when(go)
            def _():
                for e, piece in enumerate(pieces):
                    part_of = rg.at[slot, piece]
                    pltpu.make_async_copy(part_of, part_of, r_send.at[way, t, e]).wait()

    for m in range(held):
        for n in range(steps):
            piece = lg.at[m * chans + core, span(n)]
            for e in range(1, chans):
                pltpu.make_async_copy(piece, piece, l2_send.at[m, e - 1, n]).wait()

    @pl.when(is_home)
    def _():
        for m in range(held):
            for n in range(steps):
                piece = lg.at[m * chans + core, span(n)]
                for d in range(1, chips):
                    pltpu.make_async_copy(piece, piece, x_send.at[m, d - 1, n]).wait()

    for n, (a, b) in enumerate(AROUND):

        @pl.when(there(a, b))
        def _():
            piece = hsend.at[n, pl.ds(0, lines(a, b))]
            pltpu.make_async_copy(piece, piece, h_send.at[n]).wait()
    for q in range(1, stripes - 1):
        middle(q).wait()
    for copy in closing:
        copy.wait()


def on_device(
    mesh_shape,
    pair_input,
    alignment_features,
    alignment_mask,
    token_valid,
    left_weight,
    right_weight,
    output_weight,
    gate_weight,
    up_weight,
    down_weight,
    kernel_weight,
):
    rd, cd, ch = pair_input.shape
    sl, tl, aw = alignment_features.shape
    pw = left_weight.shape[1]
    hid = gate_weight.shape[1]
    rn, chans = mesh_shape["row"], mesh_shape["chan"]
    cn = mesh_shape["col"] * chans
    fold = rn // cn
    per = 128 // pw
    cr = min(16, rd)
    depth = rn * sl
    steps = rd // cr
    tall = max(rd, cd, 16)
    half = cd // 2
    seg = min(half, rd)
    subs = rd // seg
    groups, rgroups = rd // per, cd // per
    cuts = min(4, rgroups)
    held = rn // chans
    sizes = (rn, cn, chans, fold, rd, cd, ch, sl, tl, pw, cr)
    operands = (
        alignment_features,
        alignment_mask,
        token_valid.reshape(1, -1),
        left_weight.T,
        right_weight.T,
        pair_input,
        output_weight,
        gate_weight,
        up_weight,
        down_weight,
        kernel_weight.reshape(3, 3 * ch, ch),
    )
    dma = pltpu.SemaphoreType.DMA
    anywhere = pl.BlockSpec(memory_space=pl.ANY)
    return pl.pallas_call(
        functools.partial(block_kernel, sizes),
        out_shape=jax.ShapeDtypeStruct((rd, cd, ch), BF16),
        in_specs=[anywhere] * len(operands),
        out_specs=anywhere,
        scratch_shapes=[
            *[pltpu.VMEM(value.shape, value.dtype) for value in operands],
            dma((len(operands),)),
            pltpu.VMEM((2, sl * tl, 128), F32),
            pltpu.VMEM((tall, ch), F32),
            pltpu.VMEM((fold, groups + 1, sl, 128), BF16),
            pltpu.VMEM((rn, groups + 1, sl, 128), BF16),
            pltpu.VMEM((rn, rgroups + 1, sl, 128), BF16),
            pltpu.VMEM((cd * pw, depth), F32),
            pltpu.VMEM((2, pw // 2 * half, 2 * depth), BF16),
            pltpu.VMEM((2 * depth, cr * pw * 2), BF16),
            pltpu.VMEM((pw * pw, ch), F32),
            pltpu.VMEM((pw // 2 * 128, 2 * ch), BF16),
            pltpu.VMEM((2 * (cr // per) * half, pw // 2 * 128), BF16),
            pltpu.VMEM((rd, cd, ch), F32),
            pltpu.VMEM((128, 128), F32),
            pltpu.VMEM((cr, half, ch), BF16),
            pltpu.VMEM((rd, cd, ch), BF16),
            pltpu.VMEM((cd, rd, ch), BF16),
            pltpu.VMEM((cr * seg, ch), F32),
            pltpu.VMEM((rd, cd, ch), F32),
            pltpu.VMEM((rd + 2, cd, 3 * ch), BF16),
            pltpu.VMEM((2, rd, ch), F32),
            pltpu.VMEM((8, tall, ch), BF16),
            pltpu.VMEM((8, tall, ch), BF16),
            pltpu.VMEM((rd, cd, ch), BF16),
            dma((fold, steps)),
            dma((held, steps)),
            dma((held, max(cn // chans - 1, 1), steps)),
            dma((held, max(chans - 1, 1), steps)),
            dma((held, max(chans - 1, 1), steps)),
            dma((2, rn - 1, cuts)),
            dma((rn, cuts)),
            dma((fold, steps, subs)),
            dma((fold, steps, subs)),
            pltpu.VMEM((2, steps, subs, cr, seg, ch), BF16),
            dma((2, steps, subs)),
            dma((2, steps, subs)),
            dma((8,)),
            dma((8,)),
            dma((3, max(cd // cr, 2))),
        ],
        compiler_params=pltpu.CompilerParams(
            collective_id=0, has_side_effects=True, vmem_limit_bytes=44 * 1024 * 1024
        ),
    )(*[pltpu.with_memory_space_constraint(value, pltpu.HBM) for value in operands])


def solution(mesh):
    placed = (
        P(("groups", "row"), ("col", "chan"), None),
        P("row", ("groups", "col", "chan"), None),
        P("row", ("groups", "col", "chan")),
        P("groups"),
        P(),
        P(),
        P(),
        P(),
        P(),
        P(),
        P(),
    )
    return jax.shard_map(
        functools.partial(on_device, dict(mesh.shape)),
        mesh=mesh,
        in_specs=placed,
        out_specs=P(("groups", "row"), ("col", "chan"), None),
        check_vma=False,
    )
```

```python
import functools

import jax
import jax.numpy as jnp
from jax import lax
from jax.experimental import pallas as pl
from jax.experimental.pallas import tpu as pltpu
from jax.sharding import PartitionSpec as P

epsilon = 1e-05
F32, BF16 = jnp.float32, jnp.bfloat16
MESH = pl.DeviceIdType.MESH
AROUND = [(a, b) for a in (-1, 0, 1) for b in (-1, 0, 1) if (a, b) != (0, 0)]


def dot(a, b):
    return jnp.dot(a, b, preferred_element_type=F32)


def block_kernel(sizes, *refs):
    far, (out_ref, *rest) = refs[:11], refs[11:]
    near, (w_sem, *rest) = rest[:11], rest[11:]
    feat_ref, mask_ref, valid_ref, wl_ref, wr_ref = near[:5]
    pair_ref, wo_ref, wg_ref, wu_ref, wd_ref, wk_ref = near[5:]
    (
    proj,
    vrows,
    lsend,
    lg,
    rg,
    rt,
    rq,
    lcat,
    wof,
    w2,
    zs,
    rexp,
    inv,
    ones,
    two,
    mirror,
    mf,
    sym,
    wide,
    colf,
    hsend,
    hrecv,
    result,
    l1_send,
    l1_recv,
    x_send,
    e_send,
    l2_send,
    l2_recv,
    r_send,
    r_recv,
    m_send,
    m_recv,
    relay,
    rl_send,
    rl_recv,
    h_send,
    h_recv,
    o_sem,
    ) = rest
    rn, cn, chans, fold, rd, cd, ch, sl, tl, pw, cr = sizes
    row = lax.axis_index("row")
    col = lax.axis_index("col") * chans + lax.axis_index("chan")
    per = 128 // pw
    lgroups, rgroups = rd // per, cd // per
    cuts = min(3, rgroups)
    depth = rn * sl
    steps = rd // cr
    cgroups = cr // per
    half = cd // 2
    seg = min(half, rd)
    subs = rd // seg

    def at(r, c):
        return {"row": r, "col": c // chans, "chan": c % chans}

    def remote(src, dst, ssem, rsem, r, c):
        return pltpu.make_async_remote_copy(
            src_ref=src, dst_ref=dst, send_sem=ssem, recv_sem=rsem,
            device_id=at(r, c), device_id_type=MESH,
        )

    loads = [pltpu.make_async_copy(far[n], near[n], w_sem.at[n]) for n in range(11)]
    for n in (1, 3, 4, 0, 2, 6, 5, 7, 8, 9, 10):
        loads[n].start()
    barrier = pltpu.get_barrier_semaphore()

    def greet(n, carry):
        pl.semaphore_signal(barrier, inc=1, device_id=at(n // cn, n % cn), device_id_type=MESH)
        return carry

    lax.fori_loop(0, rn * cn, greet, 0)
    hrecv[...] = jnp.zeros_like(hrecv)
    for i in (0, rd + 1):
        wide[i] = jnp.zeros((cd, 3 * ch), BF16)

    spread = (
        lax.broadcasted_iota(jnp.int32, (pw, 128), 1) % pw
        == lax.broadcasted_iota(jnp.int32, (pw, 128), 0)
    ).astype(F32).astype(BF16)
    for n in (1, 3, 4):
        loads[n].wait()
    mask = mask_ref[...].astype(F32).astype(BF16)
    spots = tl // per
    token_of = (
        lax.broadcasted_iota(jnp.int32, (tl, spots * 128), 1) // pw
        == lax.broadcasted_iota(jnp.int32, (tl, spots * 128), 0)
    ).astype(F32).astype(BF16)
    wide_mask = dot(mask, token_of)
    tiles = [
        lax.dot_general(
            w_ref[...], spread, (((0,), (0,)), ((), ())), preferred_element_type=F32
        ).astype(BF16)
        for w_ref in (wl_ref, wr_ref)
    ]
    loads[0].wait()
    feats = feat_ref[...].reshape(sl * tl, feat_ref.shape[2])
    lane_of = lax.broadcasted_iota(jnp.int32, (sl, 128), 1) // pw

    def project(n):
        proj[n] = dot(feats, tiles[n])
        parts = []
        for g in range(spots):
            got = proj[n, pl.ds(g * per, sl, stride=tl), :]
            for t in range(1, per):
                other = proj[n, pl.ds(g * per + t, sl, stride=tl), :]
                got = jnp.where(lane_of == t, other, got)
            parts.append((got * wide_mask[:, g * 128 : (g + 1) * 128]).astype(BF16))
        return parts

    left = project(0)
    for k in range(fold):
        for g in range(lgroups):
            lsend[k, 1 + g] = left[k * lgroups + g]
        lsend[k, 0] = jnp.zeros((sl, 128), BF16)
        lsend[k, 0, :, 0:rd] = mask[:, k * rd : (k + 1) * rd]
    def project_right():
        right = project(1)
        for g in range(rgroups):
            rg[row, 1 + g] = right[g]
        rg[row, 0] = jnp.zeros((sl, 128), BF16)
        rg[row, 0, :, 0:tl] = mask

    early = row < rn // 2

    @pl.when(early)
    def _():
        project_right()


    pl.semaphore_wait(barrier, rn * cn)

    def span(n):
        if isinstance(n, int) and n == 0:
            return pl.ds(0, cgroups + 1)
        return pl.ds(1 + n * cgroups, cgroups)

    core, chip = col % chans, col // chans
    held = rn // chans
    home = row // fold // chans
    is_home = chip == home

    def l1_target(k):
        to_row, to_col = col * fold + k, chip * chans + row % chans
        return to_row, to_col, jnp.logical_and(to_row == row, to_col == col)

    def send_left(n):
        for k in range(fold):
            to_row, to_col, mine = l1_target(k)
            slot = row // chans
            src, dst = lsend.at[k, span(n)], lg.at[row, span(n)]

            @pl.when(mine)
            def _():
                pltpu.make_async_copy(src, dst, l1_recv.at[slot, n]).start()

            @pl.when(jnp.logical_not(mine))
            def _():
                remote(src, dst, l1_send.at[k], l1_recv.at[slot, n], to_row, to_col).start()

    chips = cn // chans

    def spread_left(i, n, at_home):
        m = (row // chans + i) % held
        first = isinstance(n, int) and n == 0
        piece = lg.at[m * chans + core, span(n)]
        pltpu.make_async_copy(piece, piece, l1_recv.at[m, n]).wait()
        if at_home:
            for d in range(1, chips):
                there_chip = (chip + d) % chips * chans
                remote(
                    piece, piece, x_send.at[d - 1], l1_recv.at[m, n], row, there_chip + core
                ).start()
                for e in range(1, chans if first else 0):
                    remote(
                        piece, piece, e_send.at[d - 1], l2_recv.at[n],
                        row, there_chip + (core + e) % chans,
                    ).start()
        for e in range(1, chans if at_home or not first else 0):
            remote(
                piece, piece, l2_send.at[0], l2_recv.at[n],
                row, chip * chans + (core + e) % chans,
            ).start()

    def take_left(n):
        got = lg.at[pl.ds(0, held * (chans - 1)), span(n)]
        pltpu.make_async_copy(got, got, l2_recv.at[n]).wait()

    send_left(0)

    @pl.when(jnp.logical_not(early))
    def _():
        project_right()

    def chain(t):
        low, high = jnp.maximum(row - t, 0), jnp.minimum(row + t, rn - 1)
        ups = jnp.logical_and(row - t >= 0, row + 1 < rn)
        downs = jnp.logical_and(row + t < rn, row >= 1)
        return (ups, low, row + 1), (downs, high, row - 1)

    quarter = max(rgroups // 4, 1)
    early_pieces = [
        pl.ds(1 + e * quarter, quarter) if e else pl.ds(0, 1 + quarter)
        for e in range(rgroups // 2 // quarter)
    ]
    pieces = early_pieces + [pl.ds(1 + rgroups // 2, rgroups - rgroups // 2)]

    upward = chip < chips // 2

    def pass_on(urgent, later):
        for way, (go, slot, to_row) in enumerate(chain(0)):

            @pl.when(jnp.logical_and(go, upward == (urgent == (way == 0))))
            def _():
                for e in cut_range(later):
                    part_of = rg.at[slot, pieces[e]]
                    remote(
                        part_of, part_of, r_send.at[way, 0], r_recv.at[slot, e], to_row, col
                    ).start()

    def cut_range(later):
        return range(cuts - 1, cuts) if later else range(cuts - 1)

    pass_on(True, False)
    pass_on(False, False)
    pass_on(True, True)
    for n in range(1, steps):
        send_left(n)

    loads[2].wait()
    tokens = valid_ref.shape[1]
    valid = valid_ref[...].astype(F32)

    def as_rows(first, count):
        hit = lax.broadcasted_iota(jnp.int32, (count, tokens), 1) == first + (
            lax.broadcasted_iota(jnp.int32, (count, tokens), 0)
        )
        chosen = jnp.where(hit, jnp.broadcast_to(valid, (count, tokens)), 0.0).astype(BF16)
        return dot(chosen, jnp.ones((tokens, ch), BF16))

    vrows[0:rd] = as_rows(row * rd, rd)
    valid_cols = as_rows(col * cd, cd)

    loads[6].wait()
    wof[...] = wo_ref[...].astype(F32)
    w2[...] = jnp.zeros_like(w2)
    for q in range(pw):
        values = wof[pl.ds(q, pw, stride=pw), :].astype(BF16)
        for i in range(2):
            begin = q // 2 * 128 + (q % 2 * 2 + i) * pw
            w2[begin : begin + pw, i * ch : (i + 1) * ch] = values

    def hop(t, way, later):
        there_is, slot = (
            (row - t - 1 >= 0, jnp.maximum(row - t - 1, 0)),
            (row + t + 1 < rn, jnp.minimum(row + t + 1, rn - 1)),
        )[way]
        for e in cut_range(later):
            piece = pieces[e]

            @pl.when(there_is)
            def _():
                part_of = rg.at[slot, piece]
                pltpu.make_async_copy(part_of, part_of, r_recv.at[slot, e]).wait()

            if t + 1 < rn - 1:
                go, _slot, to_row = chain(t + 1)[way]

                @pl.when(go)
                def _():
                    part_of = rg.at[slot, piece]
                    remote(
                        part_of, part_of, r_send.at[way, t + 1], r_recv.at[slot, e],
                        to_row, col,
                    ).start()

    def hops(first, last, urgent, later=False):

        @pl.when(upward if urgent else jnp.logical_not(upward))
        def _():
            for t in range(first, last):
                hop(t, 0, later)

        @pl.when(jnp.logical_not(upward) if urgent else upward)
        def _():
            for t in range(first, last):
                hop(t, 1, later)

    ends = jnp.logical_or(row == 0, row == rn - 1)
    inner = jnp.logical_not(ends)
    away = jnp.logical_not(is_home)

    @pl.when(is_home)
    def _():
        spread_left(0, 0, True)

    @pl.when(is_home)
    def _():
        for i in range(1, held):
            spread_left(i, 0, True)

    @pl.when(jnp.logical_and(away, ends))
    def _():
        for i in range(held):
            spread_left(i, 0, False)

    hops(0, 1, True)
    @pl.when(ends)
    def _():
        pass_on(False, True)


    hops(1, rn - 1, True)

    @pl.when(jnp.logical_and(away, inner))
    def _():
        for i in range(held):
            spread_left(i, 0, False)

    @pl.when(is_home)
    def _():
        for n in range(1, steps):
            for i in range(held):
                spread_left(i, n, True)

    @pl.when(is_home)
    def _():
        hops(0, 1, True, True)

    hops(0, rn - 1, False)

    @pl.when(inner)
    def _():
        pass_on(False, True)

    @pl.when(away)
    def _():
        hops(0, 1, True, True)

    take_left(0)
    left_mask = lg[:, 0].astype(F32).reshape(depth, 128)
    right_mask = rg[:, 0].astype(F32).reshape(depth, 128)
    counts = dot(right_mask.T.astype(BF16), left_mask.astype(BF16))
    inv[...] = 1.0 / jnp.maximum(counts, 1.0)

    def prepare(h):
        for g in range(h * rgroups // 2, (h + 1) * rgroups // 2):
            slab = rg[:, 1 + g].astype(F32).reshape(depth, 128)
            rt[g * 128 : (g + 1) * 128, :] = slab.T
        for q in range(pw):
            rq[h, q // 2 * half : (q // 2 + 1) * half, q % 2 * depth : (q % 2 + 1) * depth] = rt[
                pl.ds(h * half * pw + q, half, stride=pw), :
            ].astype(BF16)
        inverse = inv[h * half : (h + 1) * half]
        for i in range(rd):
            rexp[i, h * half : (h + 1) * half] = jnp.broadcast_to(
                inverse[:, i : i + 1], (half, ch)
            )

    prepare(0)

    for n in (5, 7, 8, 9, 10):
        loads[n].wait()

    lag = 0

    slots = 1 if chips == 2 else 2
    final = steps - 1

    def segments(h):
        found = []
        for begin in range(h * half, (h + 1) * half, seg):
            found.append((begin, begin // rd, begin % rd))
        return found

    def send_mirror(h, step):
        for begin, k, off in segments(h):
            to_row, to_col = col * fold + k, row // fold
            mine = jnp.logical_and(to_row == row, to_col == col)
            across = to_col // chans != chip
            at_end = jnp.logical_or(to_row == 0, to_row == rn - 1)
            turned = jnp.logical_and(across, at_end)
            if h == 1:
                turned = jnp.logical_and(turned, step != final)
            sub = off // seg
            src = two.at[pl.ds(step * cr, cr), pl.ds(begin, seg)]
            dst = mirror.at[pl.ds(row % fold * rd + step * cr, cr), pl.ds(off, seg)]
            rsem = m_recv.at[row % fold, step, sub]
            ssem = m_send.at[k]

            @pl.when(mine)
            def _():
                pltpu.make_async_copy(src, dst, rsem).start()

            @pl.when(turned)
            def _():
                slot = jnp.where(to_row == 0, 0, slots - 1)
                remote(
                    src, relay.at[slot, step, sub], ssem, rl_recv.at[slot, step, sub],
                    row, to_col,
                ).start()

            @pl.when(jnp.logical_not(jnp.logical_or(mine, turned)))
            def _():
                remote(src, dst, ssem, rsem, to_row, to_col).start()

    def relayed(way):
        to_row = (0, rn - 1)[way]
        active = jnp.logical_and(col == row // fold, to_row // fold // chans != chip)
        return active, to_row, way % slots

    def forward(h, step):
        for way in range(2):
            active, to_row, slot = relayed(way)
            if h == 1:
                active = jnp.logical_and(active, step != final)
            for _begin, k, off in segments(h):
                if k == to_row % fold:
                    sub = off // seg

                    @pl.when(active)
                    def _():
                        piece = relay.at[slot, step, sub]
                        pltpu.make_async_copy(piece, piece, rl_recv.at[slot, step, sub]).wait()
                        remote(
                            piece,
                            mirror.at[pl.ds(row % fold * rd + step * cr, cr), pl.ds(off, seg)],
                            rl_send.at[slot, step, sub],
                            m_recv.at[row % fold, step, sub], to_row, col,
                        ).start()

    low_lanes = lax.broadcasted_iota(jnp.int32, (depth, 128), 1) < 64

    def serve(step):
        for t in range(rn - 1):

            @pl.when(step == min(t, steps - 1))
            def _():
                for way in (0, 1):
                    if t:
                        hop(t, way, True)
                    else:

                        @pl.when(upward == (way == 1))
                        def _():
                            hop(0, way, True)

        @pl.when(jnp.logical_and(away, step + 1 < steps))
        def _():
            for i in range(held):
                spread_left(i, step + 1, False)

        @pl.when(step > 0)
        def _():
            take_left(step)

    def one_step(h, step):
        lo = h * half
        if h == 0:

            @pl.when(step > 0)
            def _():
                forward(h, step)

            serve(step)

            @pl.when(step == 0)
            def _():
                forward(h, step)

        else:
            forward(h, step)

        if h and lag:

            @pl.when(step < lag)
            def _():
                forward(h - 1, steps - lag + step)

        for g in range(cgroups):
            slab = lg[:, 1 + step * cgroups + g].astype(F32).reshape(depth, 128)
            turned = pltpu.roll(slab, 64, 1)
            for i, (first, second) in enumerate(((slab, turned), (turned, slab))):
                at_lane = (g * 2 + i) * 128
                lcat[0:depth, at_lane : at_lane + 128] = jnp.where(low_lanes, first, 0.0).astype(BF16)
                lcat[depth : 2 * depth, at_lane : at_lane + 128] = jnp.where(
                    low_lanes, 0.0, second
                ).astype(BF16)
        for g in range(cgroups):
            z = dot(rq[h], lcat[:, g * 256 : (g + 1) * 256]).astype(BF16)
            for i in range(2):
                for q in range(pw // 2):
                    begin = (i * cgroups + g) * half
                    zs[begin : begin + half, q * 128 : (q + 1) * 128] = z[
                        q * half : (q + 1) * half, i * 128 : (i + 1) * 128
                    ]
        update = dot(zs[...], w2[...])
        for g in range(cgroups):
            for i in range(per):
                at_row = step * cr + g * per + i
                begin = (i // 2 * cgroups + g) * half
                add = update[begin : begin + half, i % 2 * ch : (i % 2 + 1) * ch]
                add = add * rexp[at_row, lo : lo + half]
                ones[g * per + i] = (pair_ref[at_row, lo : lo + half].astype(F32) + add).astype(BF16)
        values = ones[...].reshape(cr * half, ch).astype(F32)
        centre = jnp.mean(values, axis=-1, keepdims=True)
        shifted = values - centre
        var = jnp.mean(jnp.square(shifted), axis=-1, keepdims=True)
        normed = (shifted * lax.rsqrt(var + epsilon)).astype(BF16)
        gate = dot(normed, wg_ref[...])
        up = dot(normed, wu_ref[...])
        halved = gate * 0.5
        hidden = ((halved + halved * jnp.tanh(halved)) * up).astype(BF16)
        done = (values + dot(hidden, wd_ref[...])).astype(BF16)
        two[pl.ds(step * cr, cr), lo : lo + half] = done.reshape(cr, half, ch)
        send_mirror(h, step)

    def run(h):
        def body(step, carry):
            one_step(h, step)
            return carry

        lax.fori_loop(0, steps, body, 0)

    run(0)
    prepare(1)
    run(1)
    for step in range(steps - lag, steps):
        forward(1, step)

    stripes = cd // cr
    place = lax.broadcasted_iota(jnp.int32, (cr, ch), 0)

    def take_mirror(sub, q):
        begin = q * cr
        k, step = begin // rd, begin % rd // cr
        top = sub * seg
        piece = mirror.at[pl.ds(begin, cr), pl.ds(top, seg)]
        pltpu.make_async_copy(piece, piece, m_recv.at[k, step, sub]).wait()
        mf[0 : cr * seg] = (
            mirror[begin : begin + cr, top : top + seg].astype(F32).reshape(cr * seg, ch)
        )
        some_cols = valid_cols[begin : begin + cr]

        def one_row(i, carry):
            other = mf[pl.ds(i - top, cr, stride=seg), :]
            half_sum = (two[i, begin : begin + cr].astype(F32) + other) * 0.5
            sym[i, begin : begin + cr] = half_sum
            masked = half_sum * some_cols * vrows[pl.ds(i, 1), :]
            wide[i + 1, begin : begin + cr, ch : 2 * ch] = masked.astype(BF16)
            before = colf[1, pl.ds(i, 1), :] if q else 0.0
            wide[i + 1, begin : begin + cr, 0:ch] = jnp.where(
                place == 0, before, pltpu.roll(masked, 1, 0)
            ).astype(BF16)
            if q:
                earlier = wide[i + 1, begin - cr : begin, ch : 2 * ch].astype(F32)
                wide[i + 1, begin - cr : begin, 2 * ch : 3 * ch] = jnp.where(
                    place == cr - 1, masked[0:1], pltpu.roll(earlier, cr - 1, 0)
                ).astype(BF16)
            else:
                colf[0, pl.ds(i, 1), :] = masked[0:1]
            if q == stripes - 1:
                wide[i + 1, begin : begin + cr, 2 * ch : 3 * ch] = jnp.where(
                    place == cr - 1, 0.0, pltpu.roll(masked, cr - 1, 0)
                ).astype(BF16)
            colf[1, pl.ds(i, 1), :] = masked[cr - 1 : cr]
            return carry

        lax.fori_loop(top, top + seg, one_row, 0, unroll=4)

    top_rows = seg // 2 if subs > 1 else 0
    blocks = [(0, top_rows)] if top_rows else []
    while (blocks[-1][1] if blocks else 0) < rd:
        first = blocks[-1][1] if blocks else 0
        blocks.append((first, min(first + 32, rd)))

    def conv_block(q, first, last):
        begin = q * cr
        count = last - first
        total = sym[first:last, begin : begin + cr].reshape(count * cr, ch)
        for a in range(3):
            window = wide[first + a : last + a, begin : begin + cr]
            total = total + dot(window.reshape(count * cr, 3 * ch), wk_ref[a])
        total = total.reshape(count, cr, ch)
        result[first:last, begin : begin + cr] = total.astype(BF16)
        if q in (0, stripes - 1):
            sym[first:last, begin : begin + cr] = total
        else:
            if first == 0:
                sym[0, begin : begin + cr] = total[0]
            if last == rd:
                sym[rd - 1, begin : begin + cr] = total[count - 1]

    def conv(q):
        for first, last in blocks[1 if top_rows else 0 :]:
            conv_block(q, first, last)
        if 0 < q < stripes - 1:
            middle(q).start()

    def middle(q):
        block = (pl.ds(1, rd - 2), pl.ds(q * cr, cr))
        return pltpu.make_async_copy(result.at[block], out_ref.at[block], o_sem.at[0])

    done = 0
    for sub in range(subs):
        for q in range(stripes):
            take_mirror(sub, q)
            if sub == 0 and top_rows and q:
                conv_block(q - 1, 0, top_rows)
            if sub == subs - 1 and 0 < q < stripes - 2:
                conv(q - 1)
                done = q
        if sub == 0 and top_rows:
            conv_block(stripes - 1, 0, top_rows)

    for n, (a, b) in enumerate(AROUND):
        if b == 0:
            hsend[n, 0:cd] = wide[1 if a < 0 else rd, :, ch : 2 * ch]
        elif a == 0:
            hsend[n, 0:rd] = colf[0 if b < 0 else 1].astype(BF16)
        else:
            corner = colf[0 if b < 0 else 1, 0:1] if a < 0 else colf[0 if b < 0 else 1, rd - 1 : rd]
            hsend[n, 0:16] = jnp.broadcast_to(corner, (16, ch)).astype(BF16)

    def there(a, b):
        r, c = row + a, col + b
        return jnp.logical_and(
            jnp.logical_and(r >= 0, r < rn), jnp.logical_and(c >= 0, c < cn)
        )

    def lines(a, b):
        return cd if b == 0 else (rd if a == 0 else 16)

    for n, (a, b) in enumerate(AROUND):

        @pl.when(there(a, b))
        def _():
            size = lines(a, b)
            remote(
                hsend.at[n, pl.ds(0, size)], hrecv.at[n, pl.ds(0, size)], h_send.at[n],
                h_recv.at[n], row + a, col + b,
            ).start()

    for q in range(done, stripes):
        conv(q)

    def take_halo(wanted):
        for n, (a, b) in enumerate(AROUND):
            if wanted(a):

                @pl.when(there(-a, -b))
                def _():
                    piece = hrecv.at[n, pl.ds(0, lines(a, b))]
                    pltpu.make_async_copy(piece, piece, h_recv.at[n]).wait()

    take_halo(lambda a: a == 0)

    slot_of = {direction: n for n, direction in enumerate(AROUND)}
    along = lax.broadcasted_iota(jnp.int32, (cd, ch), 0)
    down = lax.broadcasted_iota(jnp.int32, (rd, ch), 0)

    def edge_row(a, i):
        line = hrecv[slot_of[(a, 0)], 0:cd]
        centre = line.astype(F32)
        before = hrecv[slot_of[(a, 1)], 0:16].astype(F32)[0:1]
        after = hrecv[slot_of[(a, -1)], 0:16].astype(F32)[0:1]
        lefts = jnp.where(along == 0, before, pltpu.roll(centre, 1, 0)).astype(BF16)
        rights = jnp.where(along == cd - 1, after, pltpu.roll(centre, cd - 1, 0)).astype(BF16)
        w = 0 if a > 0 else 2
        sym[i] = sym[i] + (
            dot(lefts, wk_ref[w, 0:ch])
            + dot(line, wk_ref[w, ch : 2 * ch])
            + dot(rights, wk_ref[w, 2 * ch : 3 * ch])
        )

    def edge_col(b):
        line = hrecv[slot_of[(0, b)], 0:rd]
        centre = line.astype(F32)
        above = jnp.where(down == 0, 0.0, pltpu.roll(centre, 1, 0)).astype(BF16)
        below = jnp.where(down == rd - 1, 0.0, pltpu.roll(centre, rd - 1, 0)).astype(BF16)
        lo = 0 if b > 0 else 2 * ch
        return (
            dot(above, wk_ref[0, lo : lo + ch])
            + dot(line, wk_ref[1, lo : lo + ch])
            + dot(below, wk_ref[2, lo : lo + ch])
        )

    colf[0] = edge_col(1)
    colf[1] = edge_col(-1)
    place16 = lax.broadcasted_iota(jnp.int32, (16, ch), 0)

    def patch_row(i, carry):
        first = sym[i, 0:16] + jnp.where(place16 == 0, colf[0, pl.ds(i, 1), :], 0.0)
        if cd == 16:
            first = first + jnp.where(place16 == 15, colf[1, pl.ds(i, 1), :], 0.0)
        result[i, 0:16] = first.astype(BF16)
        if cd > 16:
            result[i, cd - 16 : cd] = (
                sym[i, cd - 16 : cd] + jnp.where(place16 == 15, colf[1, pl.ds(i, 1), :], 0.0)
            ).astype(BF16)
        return carry

    lax.fori_loop(1, rd - 1, patch_row, 0, unroll=2)

    for n, q in enumerate((0, stripes - 1)):
        block = (pl.ds(1, rd - 2), pl.ds(q * cr, cr))
        pltpu.make_async_copy(result.at[block], out_ref.at[block], o_sem.at[2]).start()

    take_halo(lambda a: a != 0)
    for a, i in ((1, 0), (-1, rd - 1)):
        edge_row(a, i)
        total = sym[i]
        total = total + jnp.where(along == 0, colf[0, i : i + 1, :], 0.0)
        total = total + jnp.where(along == cd - 1, colf[1, i : i + 1, :], 0.0)
        result[i] = total.astype(BF16)
        pltpu.make_async_copy(result.at[i], out_ref.at[i], o_sem.at[1]).start()

    for k in range(fold):
        @pl.when(jnp.logical_not(l1_target(k)[2]))
        def _():
            pltpu.make_async_copy(lsend.at[k], lsend.at[k], l1_send.at[k]).wait()

        to_row, to_col = col * fold + k, row // fold

        @pl.when(jnp.logical_not(jnp.logical_and(to_row == row, to_col == col)))
        def _():
            src = two.at[pl.ds(0, rd), pl.ds(k * rd, rd)]
            pltpu.make_async_copy(src, src, m_send.at[k]).wait()

    for way in range(2):
        active, to_row, slot = relayed(way)
        for h in range(2):
            for _begin, k, off in segments(h):
                count = steps - 1 if h == 1 else steps
                if k == to_row % fold and count:

                    @pl.when(active)
                    def _():
                        for step in range(count):
                            piece = relay.at[slot, step, off // seg]
                            pltpu.make_async_copy(
                                piece, piece, rl_send.at[slot, step, off // seg]
                            ).wait()

    for t in range(rn - 1):
        for way, (go, slot, _to_row) in enumerate(chain(t)):

            @pl.when(go)
            def _():
                pltpu.make_async_copy(rg.at[slot], rg.at[slot], r_send.at[way, t]).wait()

    others = pl.ds(0, held * (chans - 1))
    if steps > 1:

        @pl.when(away)
        def _():
            got = lg.at[others, pl.ds(1 + cgroups, (steps - 1) * cgroups)]
            pltpu.make_async_copy(got, got, l2_send.at[0]).wait()

    @pl.when(is_home)
    def _():
        pltpu.make_async_copy(lg.at[others], lg.at[others], l2_send.at[0]).wait()
        for d in range(1, chips):
            got = lg.at[pl.ds(0, held)]
            pltpu.make_async_copy(got, got, x_send.at[d - 1]).wait()
            got = lg.at[others, span(0)]
            pltpu.make_async_copy(got, got, e_send.at[d - 1]).wait()

    for n, (a, b) in enumerate(AROUND):

        @pl.when(there(a, b))
        def _():
            piece = hsend.at[n, pl.ds(0, lines(a, b))]
            pltpu.make_async_copy(piece, piece, h_send.at[n]).wait()
    if stripes > 2:
        block = (pl.ds(1, rd - 2), pl.ds(cr, cd - 2 * cr))
        pltpu.make_async_copy(result.at[block], out_ref.at[block], o_sem.at[0]).wait()
    block = pl.ds(0, 2)
    pltpu.make_async_copy(result.at[block], out_ref.at[block], o_sem.at[1]).wait()
    block = (pl.ds(1, rd - 2), pl.ds(0, 2 * cr))
    pltpu.make_async_copy(result.at[block], out_ref.at[block], o_sem.at[2]).wait()


def on_device(
    mesh_shape,
    pair_input,
    alignment_features,
    alignment_mask,
    token_valid,
    left_weight,
    right_weight,
    output_weight,
    gate_weight,
    up_weight,
    down_weight,
    kernel_weight,
):
    rd, cd, ch = pair_input.shape
    sl, tl, aw = alignment_features.shape
    pw = left_weight.shape[1]
    hid = gate_weight.shape[1]
    rn, chans = mesh_shape["row"], mesh_shape["chan"]
    cn = mesh_shape["col"] * chans
    fold = rn // cn
    per = 128 // pw
    cr = min(16, rd)
    depth = rn * sl
    steps = rd // cr
    tall = max(rd, cd, 16)
    half = cd // 2
    seg = min(half, rd)
    subs = rd // seg
    groups, rgroups = rd // per, cd // per
    cuts = min(3, rgroups)
    held = rn // chans
    slots = 1 if cn // chans == 2 else 2
    sizes = (rn, cn, chans, fold, rd, cd, ch, sl, tl, pw, cr)
    operands = (
        alignment_features,
        alignment_mask,
        token_valid.reshape(1, -1),
        left_weight.T,
        right_weight.T,
        pair_input,
        output_weight,
        gate_weight,
        up_weight,
        down_weight,
        kernel_weight.reshape(3, 3 * ch, ch),
    )
    dma = pltpu.SemaphoreType.DMA
    anywhere = pl.BlockSpec(memory_space=pl.ANY)
    return pl.pallas_call(
        functools.partial(block_kernel, sizes),
        out_shape=jax.ShapeDtypeStruct((rd, cd, ch), BF16),
        in_specs=[anywhere] * len(operands),
        out_specs=anywhere,
        scratch_shapes=[
            *[pltpu.VMEM(value.shape, value.dtype) for value in operands],
            dma((len(operands),)),
            pltpu.VMEM((2, sl * tl, 128), F32),
            pltpu.VMEM((tall, ch), F32),
            pltpu.VMEM((fold, groups + 1, sl, 128), BF16),
            pltpu.VMEM((rn, groups + 1, sl, 128), BF16),
            pltpu.VMEM((rn, rgroups + 1, sl, 128), BF16),
            pltpu.VMEM((cd * pw, depth), F32),
            pltpu.VMEM((2, pw // 2 * half, 2 * depth), BF16),
            pltpu.VMEM((2 * depth, cr * pw * 2), BF16),
            pltpu.VMEM((pw * pw, ch), F32),
            pltpu.VMEM((pw // 2 * 128, 2 * ch), BF16),
            pltpu.VMEM((2 * (cr // per) * half, pw // 2 * 128), BF16),
            pltpu.VMEM((rd, cd, ch), F32),
            pltpu.VMEM((128, 128), F32),
            pltpu.VMEM((cr, half, ch), BF16),
            pltpu.VMEM((rd, cd, ch), BF16),
            pltpu.VMEM((cd, rd, ch), BF16),
            pltpu.VMEM((cr * seg, ch), F32),
            pltpu.VMEM((rd, cd, ch), F32),
            pltpu.VMEM((rd + 2, cd, 3 * ch), BF16),
            pltpu.VMEM((2, rd, ch), F32),
            pltpu.VMEM((8, tall, ch), BF16),
            pltpu.VMEM((8, tall, ch), BF16),
            pltpu.VMEM((rd, cd, ch), BF16),
            dma((fold,)),
            dma((held, steps)),
            dma((max(cn // chans - 1, 1),)),
            dma((max(cn // chans - 1, 1),)),
            dma((1,)),
            dma((steps,)),
            dma((2, rn - 1)),
            dma((rn, cuts)),
            dma((fold,)),
            dma((fold, steps, subs)),
            pltpu.VMEM((slots, steps, subs, cr, seg, ch), BF16),
            dma((slots, steps, subs)),
            dma((slots, steps, subs)),
            dma((8,)),
            dma((8,)),
            dma((3,)),
        ],
        compiler_params=pltpu.CompilerParams(
            collective_id=0, has_side_effects=True, vmem_limit_bytes=44 * 1024 * 1024
        ),
    )(*[pltpu.with_memory_space_constraint(value, pltpu.HBM) for value in operands])


def solution(mesh):
    placed = (
        P(("groups", "row"), ("col", "chan"), None),
        P("row", ("groups", "col", "chan"), None),
        P("row", ("groups", "col", "chan")),
        P("groups"),
        P(),
        P(),
        P(),
        P(),
        P(),
        P(),
        P(),
    )
    return jax.shard_map(
        functools.partial(on_device, dict(mesh.shape)),
        mesh=mesh,
        in_specs=placed,
        out_specs=P(("groups", "row"), ("col", "chan"), None),
        check_vma=False,
    )
```

```python
import functools

import jax
import jax.numpy as jnp
from jax import lax
from jax.experimental import pallas as pl
from jax.experimental.pallas import tpu as pltpu
from jax.sharding import PartitionSpec as P

epsilon = 1e-05
F32, BF16 = jnp.float32, jnp.bfloat16
MESH = pl.DeviceIdType.MESH
AROUND = [(a, b) for a in (-1, 0, 1) for b in (-1, 0, 1) if (a, b) != (0, 0)]


def dot(a, b):
    return jnp.dot(a, b, preferred_element_type=F32)


def block_kernel(sizes, *refs):
    far, (out_ref, *rest) = refs[:11], refs[11:]
    near, (w_sem, *rest) = rest[:11], rest[11:]
    feat_ref, mask_ref, valid_ref, wl_ref, wr_ref = near[:5]
    pair_ref, wo_ref, wg_ref, wu_ref, wd_ref, wk_ref = near[5:]
    (
    proj,
    vrows,
    lsend,
    lg,
    rg,
    rt,
    rq,
    lcat,
    wof,
    w2,
    zs,
    rexp,
    inv,
    ones,
    two,
    mirror,
    mf,
    sym,
    wide,
    colf,
    hsend,
    hrecv,
    result,
    l1_send,
    l1_recv,
    x_send,
    e_send,
    l2_send,
    l2_recv,
    r_send,
    r_recv,
    m_send,
    m_recv,
    relay,
    extra,
    ex_send,
    ex_recv,
    rl_send,
    rl_recv,
    h_send,
    h_recv,
    o_sem,
    ) = rest
    rn, cn, chans, fold, rd, cd, ch, sl, tl, pw, cr = sizes
    row = lax.axis_index("row")
    col = lax.axis_index("col") * chans + lax.axis_index("chan")
    per = 128 // pw
    lgroups, rgroups = rd // per, cd // per
    cuts = min(3, rgroups)
    depth = rn * sl
    steps = rd // cr
    cgroups = cr // per
    half = cd // 2
    seg = min(half, rd)
    subs = rd // seg

    def at(r, c):
        return {"row": r, "col": c // chans, "chan": c % chans}

    def remote(src, dst, ssem, rsem, r, c):
        return pltpu.make_async_remote_copy(
            src_ref=src, dst_ref=dst, send_sem=ssem, recv_sem=rsem,
            device_id=at(r, c), device_id_type=MESH,
        )

    loads = [pltpu.make_async_copy(far[n], near[n], w_sem.at[n]) for n in range(11)]
    for n in (1, 3, 4, 0, 2, 6, 5, 7, 8, 9, 10):
        loads[n].start()
    barrier = pltpu.get_barrier_semaphore()

    def greet(n, carry):
        pl.semaphore_signal(barrier, inc=1, device_id=at(n // cn, n % cn), device_id_type=MESH)
        return carry

    lax.fori_loop(0, rn * cn, greet, 0)
    hrecv[...] = jnp.zeros_like(hrecv)
    for i in (0, rd + 1):
        wide[i] = jnp.zeros((cd, 3 * ch), BF16)

    spread = (
        lax.broadcasted_iota(jnp.int32, (pw, 128), 1) % pw
        == lax.broadcasted_iota(jnp.int32, (pw, 128), 0)
    ).astype(F32).astype(BF16)
    for n in (1, 3, 4):
        loads[n].wait()
    mask = mask_ref[...].astype(F32).astype(BF16)
    spots = tl // per
    token_of = (
        lax.broadcasted_iota(jnp.int32, (tl, spots * 128), 1) // pw
        == lax.broadcasted_iota(jnp.int32, (tl, spots * 128), 0)
    ).astype(F32).astype(BF16)
    wide_mask = dot(mask, token_of)
    tiles = [
        lax.dot_general(
            w_ref[...], spread, (((0,), (0,)), ((), ())), preferred_element_type=F32
        ).astype(BF16)
        for w_ref in (wl_ref, wr_ref)
    ]
    loads[0].wait()
    feats = feat_ref[...].reshape(sl * tl, feat_ref.shape[2])
    lane_of = lax.broadcasted_iota(jnp.int32, (sl, 128), 1) // pw

    def project(n):
        proj[n] = dot(feats, tiles[n])
        parts = []
        for g in range(spots):
            got = proj[n, pl.ds(g * per, sl, stride=tl), :]
            for t in range(1, per):
                other = proj[n, pl.ds(g * per + t, sl, stride=tl), :]
                got = jnp.where(lane_of == t, other, got)
            parts.append((got * wide_mask[:, g * 128 : (g + 1) * 128]).astype(BF16))
        return parts

    left = project(0)
    for k in range(fold):
        for g in range(lgroups):
            lsend[k, 1 + g] = left[k * lgroups + g]
        lsend[k, 0] = jnp.zeros((sl, 128), BF16)
        lsend[k, 0, :, 0:rd] = mask[:, k * rd : (k + 1) * rd]
    def project_right():
        right = project(1)
        for g in range(rgroups):
            rg[row, 1 + g] = right[g]
        rg[row, 0] = jnp.zeros((sl, 128), BF16)
        rg[row, 0, :, 0:tl] = mask

    early = row < rn // 2

    @pl.when(early)
    def _():
        project_right()


    pl.semaphore_wait(barrier, rn * cn)

    def span(n):
        if isinstance(n, int) and n == 0:
            return pl.ds(0, cgroups + 1)
        return pl.ds(1 + n * cgroups, cgroups)

    core, chip = col % chans, col // chans
    held = rn // chans
    home = row // fold // chans
    is_home = chip == home

    def l1_target(k):
        to_row, to_col = col * fold + k, chip * chans + row % chans
        return to_row, to_col, jnp.logical_and(to_row == row, to_col == col)

    def send_left(n):
        for k in range(fold):
            to_row, to_col, mine = l1_target(k)
            slot = row // chans
            src, dst = lsend.at[k, span(n)], lg.at[row, span(n)]

            @pl.when(mine)
            def _():
                pltpu.make_async_copy(src, dst, l1_recv.at[slot, n]).start()

            @pl.when(jnp.logical_not(mine))
            def _():
                remote(src, dst, l1_send.at[k], l1_recv.at[slot, n], to_row, to_col).start()

    chips = cn // chans

    def spread_left(i, n, at_home):
        m = (row // chans + i) % held
        first = isinstance(n, int) and n == 0
        piece = lg.at[m * chans + core, span(n)]
        pltpu.make_async_copy(piece, piece, l1_recv.at[m, n]).wait()
        if at_home:
            for d in range(1, chips):
                there_chip = (chip + d) % chips * chans
                remote(
                    piece, piece, x_send.at[d - 1], l1_recv.at[m, n], row, there_chip + core
                ).start()
                for e in range(1, chans if first else 0):
                    remote(
                        piece, piece, e_send.at[d - 1], l2_recv.at[n],
                        row, there_chip + (core + e) % chans,
                    ).start()
        for e in range(1, chans if at_home or not first else 0):
            remote(
                piece, piece, l2_send.at[0], l2_recv.at[n],
                row, chip * chans + (core + e) % chans,
            ).start()

    def take_left(n):
        got = lg.at[pl.ds(0, held * (chans - 1)), span(n)]
        pltpu.make_async_copy(got, got, l2_recv.at[n]).wait()

    send_left(0)

    @pl.when(jnp.logical_not(early))
    def _():
        project_right()

    def chain(t):
        low, high = jnp.maximum(row - t, 0), jnp.minimum(row + t, rn - 1)
        ups = jnp.logical_and(row - t >= 0, row + 1 < rn)
        downs = jnp.logical_and(row + t < rn, row >= 1)
        return (ups, low, row + 1), (downs, high, row - 1)

    quarter = max(rgroups // 4, 1)
    early_pieces = [
        pl.ds(1 + e * quarter, quarter) if e else pl.ds(0, 1 + quarter)
        for e in range(rgroups // 2 // quarter)
    ]
    pieces = early_pieces + [pl.ds(1 + rgroups // 2, rgroups - rgroups // 2)]

    upward = chip < chips // 2

    def pass_on(urgent, later):
        for way, (go, slot, to_row) in enumerate(chain(0)):

            @pl.when(jnp.logical_and(go, upward == (urgent == (way == 0))))
            def _():
                for e in cut_range(later):
                    part_of = rg.at[slot, pieces[e]]
                    remote(
                        part_of, part_of, r_send.at[way, 0], r_recv.at[slot, e], to_row, col
                    ).start()

    def cut_range(later):
        return range(cuts - 1, cuts) if later else range(cuts - 1)

    pass_on(True, False)
    pass_on(False, False)
    pass_on(True, True)
    for n in range(1, steps):
        send_left(n)

    loads[2].wait()
    tokens = valid_ref.shape[1]
    valid = valid_ref[...].astype(F32)

    def as_rows(first, count):
        hit = lax.broadcasted_iota(jnp.int32, (count, tokens), 1) == first + (
            lax.broadcasted_iota(jnp.int32, (count, tokens), 0)
        )
        chosen = jnp.where(hit, jnp.broadcast_to(valid, (count, tokens)), 0.0).astype(BF16)
        return dot(chosen, jnp.ones((tokens, ch), BF16))

    vrows[0:rd] = as_rows(row * rd, rd)
    valid_cols = as_rows(col * cd, cd)

    loads[6].wait()
    wof[...] = wo_ref[...].astype(F32)
    w2[...] = jnp.zeros_like(w2)
    for q in range(pw):
        values = wof[pl.ds(q, pw, stride=pw), :].astype(BF16)
        for i in range(2):
            begin = q // 2 * 128 + (q % 2 * 2 + i) * pw
            w2[begin : begin + pw, i * ch : (i + 1) * ch] = values

    def hop(t, way, later):
        there_is, slot = (
            (row - t - 1 >= 0, jnp.maximum(row - t - 1, 0)),
            (row + t + 1 < rn, jnp.minimum(row + t + 1, rn - 1)),
        )[way]
        for e in cut_range(later):
            piece = pieces[e]

            @pl.when(there_is)
            def _():
                part_of = rg.at[slot, piece]
                pltpu.make_async_copy(part_of, part_of, r_recv.at[slot, e]).wait()

            if t + 1 < rn - 1:
                go, _slot, to_row = chain(t + 1)[way]

                @pl.when(go)
                def _():
                    part_of = rg.at[slot, piece]
                    remote(
                        part_of, part_of, r_send.at[way, t + 1], r_recv.at[slot, e],
                        to_row, col,
                    ).start()

    def hops(first, last, urgent, later=False):

        @pl.when(upward if urgent else jnp.logical_not(upward))
        def _():
            for t in range(first, last):
                hop(t, 0, later)

        @pl.when(jnp.logical_not(upward) if urgent else upward)
        def _():
            for t in range(first, last):
                hop(t, 1, later)

    ends = jnp.logical_or(row == 0, row == rn - 1)
    inner = jnp.logical_not(ends)
    away = jnp.logical_not(is_home)

    @pl.when(is_home)
    def _():
        spread_left(0, 0, True)

    @pl.when(is_home)
    def _():
        for i in range(1, held):
            spread_left(i, 0, True)

    @pl.when(jnp.logical_and(away, ends))
    def _():
        for i in range(held):
            spread_left(i, 0, False)

    hops(0, 1, True)
    @pl.when(ends)
    def _():
        pass_on(False, True)


    hops(0, 1, False)

    hops(1, rn - 1, True)

    @pl.when(jnp.logical_and(away, inner))
    def _():
        for i in range(held):
            spread_left(i, 0, False)

    @pl.when(is_home)
    def _():
        for n in range(1, steps):
            for i in range(held):
                spread_left(i, n, True)

    @pl.when(is_home)
    def _():
        hops(0, 1, True, True)

    hops(1, rn - 1, False)

    @pl.when(inner)
    def _():
        pass_on(False, True)

    @pl.when(away)
    def _():
        hops(0, 1, True, True)

    take_left(0)
    left_mask = lg[:, 0].astype(F32).reshape(depth, 128)
    right_mask = rg[:, 0].astype(F32).reshape(depth, 128)
    counts = dot(right_mask.T.astype(BF16), left_mask.astype(BF16))
    inv[...] = 1.0 / jnp.maximum(counts, 1.0)

    def prepare(h):
        for g in range(h * rgroups // 2, (h + 1) * rgroups // 2):
            slab = rg[:, 1 + g].astype(F32).reshape(depth, 128)
            rt[g * 128 : (g + 1) * 128, :] = slab.T
        for q in range(pw):
            rq[h, q // 2 * half : (q // 2 + 1) * half, q % 2 * depth : (q % 2 + 1) * depth] = rt[
                pl.ds(h * half * pw + q, half, stride=pw), :
            ].astype(BF16)
        inverse = inv[h * half : (h + 1) * half]
        for i in range(rd):
            rexp[i, h * half : (h + 1) * half] = jnp.broadcast_to(
                inverse[:, i : i + 1], (half, ch)
            )

    prepare(0)

    for n in (5, 7, 8, 9, 10):
        loads[n].wait()

    lag = 0

    slots = 1 if chips == 2 else 2
    final = steps - 1

    def segments(h):
        found = []
        for begin in range(h * half, (h + 1) * half, seg):
            found.append((begin, begin // rd, begin % rd))
        return found

    def send_mirror(h, step):
        for g, (begin, k, off) in enumerate(segments(h)):
            to_row, to_col = col * fold + k, row // fold
            mine = jnp.logical_and(to_row == row, to_col == col)
            across = to_col // chans != chip
            at_end = jnp.logical_or(to_row == 0, to_row == rn - 1)
            turned = jnp.logical_and(across, at_end)
            if h == 1:
                turned = jnp.logical_and(turned, step != final)
            bent = jnp.logical_and(across, jnp.logical_not(at_end))
            bent = bent & inner & jnp.logical_not(upward)
            bent = jnp.logical_and(bent, step == 0) if h == 1 else False
            sub = off // seg
            src = two.at[pl.ds(step * cr, cr), pl.ds(begin, seg)]
            dst = mirror.at[pl.ds(row % fold * rd + step * cr, cr), pl.ds(off, seg)]
            rsem = m_recv.at[row % fold, step, sub]
            ssem = m_send.at[k]

            @pl.when(mine)
            def _():
                pltpu.make_async_copy(src, dst, rsem).start()

            @pl.when(turned)
            def _():
                slot = jnp.where(to_row == 0, 0, slots - 1)
                remote(
                    src, relay.at[slot, step, sub], ssem, rl_recv.at[slot, step, sub],
                    row, to_col,
                ).start()

            if h == 1:

                @pl.when(bent)
                def _():
                    slot = (col + 2 * cn - (to_col // chans + 1) * chans) % cn
                    remote(
                        src, extra.at[slot, g], ssem, ex_recv.at[slot, g], row, to_col
                    ).start()

            @pl.when(jnp.logical_not(mine | turned | bent))
            def _():
                remote(src, dst, ssem, rsem, to_row, to_col).start()

    def relayed(way):
        to_row = (0, rn - 1)[way]
        active = jnp.logical_and(col == row // fold, to_row // fold // chans != chip)
        return active, to_row, way % slots

    def forward(h, step):
        for way in range(2):
            active, to_row, slot = relayed(way)
            if h == 1:
                active = jnp.logical_and(active, step != final)
            for _begin, k, off in segments(h):
                if k == to_row % fold:
                    sub = off // seg

                    @pl.when(active)
                    def _():
                        piece = relay.at[slot, step, sub]
                        pltpu.make_async_copy(piece, piece, rl_recv.at[slot, step, sub]).wait()
                        remote(
                            piece,
                            mirror.at[pl.ds(row % fold * rd + step * cr, cr), pl.ds(off, seg)],
                            rl_send.at[slot, step, sub],
                            m_recv.at[row % fold, step, sub], to_row, col,
                        ).start()

    def bend():
        for slot in range(cn - chans):
            from_col = ((chip + 1) * chans + slot) % cn
            for g, (_begin, k, off) in enumerate(segments(1)):
                to_row = from_col * fold + k
                active = (col == row // fold) & inner & (to_row != 0) & (to_row != rn - 1)
                active = active & (from_col // chans >= chips // 2)

                @pl.when(active)
                def _():
                    piece = extra.at[slot, g]
                    pltpu.make_async_copy(piece, piece, ex_recv.at[slot, g]).wait()
                    remote(
                        piece, mirror.at[pl.ds(row % fold * rd, cr), pl.ds(off, seg)],
                        ex_send.at[slot, g], m_recv.at[row % fold, 0, off // seg],
                        to_row, col,
                    ).start()

    def unbend():
        for slot in range(cn - chans):
            from_col = ((chip + 1) * chans + slot) % cn
            for g, (_begin, k, _off) in enumerate(segments(1)):
                to_row = from_col * fold + k
                active = (col == row // fold) & inner & (to_row != 0) & (to_row != rn - 1)
                active = active & (from_col // chans >= chips // 2)

                @pl.when(active)
                def _():
                    piece = extra.at[slot, g]
                    pltpu.make_async_copy(piece, piece, ex_send.at[slot, g]).wait()

    low_lanes = lax.broadcasted_iota(jnp.int32, (depth, 128), 1) < 64

    def serve(step):
        for t in range(rn - 1):

            @pl.when(step == jnp.where(ends, steps - 1, min(t, steps - 1)))
            def _():
                for way in (0, 1):
                    if t:
                        hop(t, way, True)
                    else:

                        @pl.when(upward == (way == 1))
                        def _():
                            hop(0, way, True)

        @pl.when(jnp.logical_and(away, step + 1 < steps))
        def _():
            for i in range(held):
                spread_left(i, step + 1, False)

        @pl.when(step > 0)
        def _():
            take_left(step)

    def one_step(h, step):
        lo = h * half
        if h == 0:

            @pl.when(inner & (step > 0))
            def _():
                forward(h, step)

            serve(step)

            @pl.when(inner & (step == 0))
            def _():
                forward(h, step)

        else:

            @pl.when(inner)
            def _():
                forward(h, step)

            @pl.when(step == min(2, steps - 1))
            def _():
                bend()


        if h and lag:

            @pl.when(step < lag)
            def _():
                forward(h - 1, steps - lag + step)

        for g in range(cgroups):
            slab = lg[:, 1 + step * cgroups + g].astype(F32).reshape(depth, 128)
            turned = pltpu.roll(slab, 64, 1)
            for i, (first, second) in enumerate(((slab, turned), (turned, slab))):
                at_lane = (g * 2 + i) * 128
                lcat[0:depth, at_lane : at_lane + 128] = jnp.where(low_lanes, first, 0.0).astype(BF16)
                lcat[depth : 2 * depth, at_lane : at_lane + 128] = jnp.where(
                    low_lanes, 0.0, second
                ).astype(BF16)
        for g in range(cgroups):
            z = dot(rq[h], lcat[:, g * 256 : (g + 1) * 256]).astype(BF16)
            for i in range(2):
                for q in range(pw // 2):
                    begin = (i * cgroups + g) * half
                    zs[begin : begin + half, q * 128 : (q + 1) * 128] = z[
                        q * half : (q + 1) * half, i * 128 : (i + 1) * 128
                    ]
        update = dot(zs[...], w2[...])
        for g in range(cgroups):
            for i in range(per):
                at_row = step * cr + g * per + i
                begin = (i // 2 * cgroups + g) * half
                add = update[begin : begin + half, i % 2 * ch : (i % 2 + 1) * ch]
                add = add * rexp[at_row, lo : lo + half]
                ones[g * per + i] = (pair_ref[at_row, lo : lo + half].astype(F32) + add).astype(BF16)
        values = ones[...].reshape(cr * half, ch).astype(F32)
        centre = jnp.mean(values, axis=-1, keepdims=True)
        shifted = values - centre
        var = jnp.mean(jnp.square(shifted), axis=-1, keepdims=True)
        normed = (shifted * lax.rsqrt(var + epsilon)).astype(BF16)
        gate = dot(normed, wg_ref[...])
        up = dot(normed, wu_ref[...])
        halved = gate * 0.5
        hidden = ((halved + halved * jnp.tanh(halved)) * up).astype(BF16)
        done = (values + dot(hidden, wd_ref[...])).astype(BF16)
        two[pl.ds(step * cr, cr), lo : lo + half] = done.reshape(cr, half, ch)
        send_mirror(h, step)

        @pl.when(ends)
        def _():
            forward(h, step)


    def run(h):
        def body(step, carry):
            one_step(h, step)
            return carry

        lax.fori_loop(0, steps, body, 0)

    run(0)
    prepare(1)
    run(1)
    for step in range(steps - lag, steps):
        forward(1, step)

    stripes = cd // cr
    place = lax.broadcasted_iota(jnp.int32, (cr, ch), 0)

    def take_mirror(sub, q):
        begin = q * cr
        k, step = begin // rd, begin % rd // cr
        top = sub * seg
        piece = mirror.at[pl.ds(begin, cr), pl.ds(top, seg)]
        pltpu.make_async_copy(piece, piece, m_recv.at[k, step, sub]).wait()
        mf[0 : cr * seg] = (
            mirror[begin : begin + cr, top : top + seg].astype(F32).reshape(cr * seg, ch)
        )
        some_cols = valid_cols[begin : begin + cr]

        def one_row(i, carry):
            other = mf[pl.ds(i - top, cr, stride=seg), :]
            half_sum = (two[i, begin : begin + cr].astype(F32) + other) * 0.5
            sym[i, begin : begin + cr] = half_sum
            masked = half_sum * some_cols * vrows[pl.ds(i, 1), :]
            wide[i + 1, begin : begin + cr, ch : 2 * ch] = masked.astype(BF16)
            before = colf[1, pl.ds(i, 1), :] if q else 0.0
            wide[i + 1, begin : begin + cr, 0:ch] = jnp.where(
                place == 0, before, pltpu.roll(masked, 1, 0)
            ).astype(BF16)
            if q:
                earlier = wide[i + 1, begin - cr : begin, ch : 2 * ch].astype(F32)
                wide[i + 1, begin - cr : begin, 2 * ch : 3 * ch] = jnp.where(
                    place == cr - 1, masked[0:1], pltpu.roll(earlier, cr - 1, 0)
                ).astype(BF16)
            else:
                colf[0, pl.ds(i, 1), :] = masked[0:1]
            if q == stripes - 1:
                wide[i + 1, begin : begin + cr, 2 * ch : 3 * ch] = jnp.where(
                    place == cr - 1, 0.0, pltpu.roll(masked, cr - 1, 0)
                ).astype(BF16)
            colf[1, pl.ds(i, 1), :] = masked[cr - 1 : cr]
            return carry

        lax.fori_loop(top, top + seg, one_row, 0, unroll=4)

    top_rows = seg // 2 if subs > 1 else 0
    blocks = [(0, top_rows)] if top_rows else []
    while (blocks[-1][1] if blocks else 0) < rd:
        first = blocks[-1][1] if blocks else 0
        blocks.append((first, min(first + 32, rd)))

    def conv_block(q, first, last):
        begin = q * cr
        count = last - first
        total = sym[first:last, begin : begin + cr].reshape(count * cr, ch)
        for a in range(3):
            window = wide[first + a : last + a, begin : begin + cr]
            total = total + dot(window.reshape(count * cr, 3 * ch), wk_ref[a])
        total = total.reshape(count, cr, ch)
        result[first:last, begin : begin + cr] = total.astype(BF16)
        if q in (0, stripes - 1):
            sym[first:last, begin : begin + cr] = total
        else:
            if first == 0:
                sym[0, begin : begin + cr] = total[0]
            if last == rd:
                sym[rd - 1, begin : begin + cr] = total[count - 1]

    def conv(q):
        for first, last in blocks[1 if top_rows else 0 :]:
            conv_block(q, first, last)
        if 0 < q < stripes - 1:
            middle(q).start()

    def middle(q):
        block = (pl.ds(1, rd - 2), pl.ds(q * cr, cr))
        return pltpu.make_async_copy(result.at[block], out_ref.at[block], o_sem.at[0])

    def there(a, b):
        r, c = row + a, col + b
        return jnp.logical_and(
            jnp.logical_and(r >= 0, r < rn), jnp.logical_and(c >= 0, c < cn)
        )

    def lines(a, b):
        return cd if b == 0 else (rd if a == 0 else 16)

    def send_halo(ready):
        for n, (a, b) in enumerate(AROUND):
            if not ready(a, b):
                continue
            size = lines(a, b)
            side = 0 if b < 0 else 1
            if b == 0:
                hsend[n, 0:cd] = wide[1 if a < 0 else rd, :, ch : 2 * ch]
            elif a == 0:
                hsend[n, 0:rd] = colf[side].astype(BF16)
            else:
                corner = colf[side, 0:1] if a < 0 else colf[side, rd - 1 : rd]
                hsend[n, 0:16] = jnp.broadcast_to(corner, (16, ch)).astype(BF16)

            @pl.when(there(a, b))
            def _():
                remote(
                    hsend.at[n, pl.ds(0, size)], hrecv.at[n, pl.ds(0, size)], h_send.at[n],
                    h_recv.at[n], row + a, col + b,
                ).start()

    done = 0
    for sub in range(subs):
        for q in range(stripes):
            take_mirror(sub, q)
            if sub == subs - 1 and q == 0:
                send_halo(lambda a, b: b < 0 and a >= 0)
            if sub == 0 and top_rows and q:
                conv_block(q - 1, 0, top_rows)
            if sub == subs - 1 and 0 < q < stripes - 2:
                conv(q - 1)
                done = q
        if sub == 0 and subs > 1:
            send_halo(lambda a, b: a < 0)
        if sub == 0 and top_rows:
            conv_block(stripes - 1, 0, top_rows)

    send_halo(lambda a, b: not (a < 0 and subs > 1) and not (b < 0 and a >= 0))

    for q in range(done, stripes):
        conv(q)

    def take_halo(wanted):
        for n, (a, b) in enumerate(AROUND):
            if wanted(a):

                @pl.when(there(-a, -b))
                def _():
                    piece = hrecv.at[n, pl.ds(0, lines(a, b))]
                    pltpu.make_async_copy(piece, piece, h_recv.at[n]).wait()

    take_halo(lambda a: a == 0)

    slot_of = {direction: n for n, direction in enumerate(AROUND)}
    along = lax.broadcasted_iota(jnp.int32, (cd, ch), 0)
    down = lax.broadcasted_iota(jnp.int32, (rd, ch), 0)

    def edge_row(a, i):
        line = hrecv[slot_of[(a, 0)], 0:cd]
        centre = line.astype(F32)
        before = hrecv[slot_of[(a, 1)], 0:16].astype(F32)[0:1]
        after = hrecv[slot_of[(a, -1)], 0:16].astype(F32)[0:1]
        lefts = jnp.where(along == 0, before, pltpu.roll(centre, 1, 0)).astype(BF16)
        rights = jnp.where(along == cd - 1, after, pltpu.roll(centre, cd - 1, 0)).astype(BF16)
        w = 0 if a > 0 else 2
        sym[i] = sym[i] + (
            dot(lefts, wk_ref[w, 0:ch])
            + dot(line, wk_ref[w, ch : 2 * ch])
            + dot(rights, wk_ref[w, 2 * ch : 3 * ch])
        )

    def edge_col(b):
        line = hrecv[slot_of[(0, b)], 0:rd]
        centre = line.astype(F32)
        above = jnp.where(down == 0, 0.0, pltpu.roll(centre, 1, 0)).astype(BF16)
        below = jnp.where(down == rd - 1, 0.0, pltpu.roll(centre, rd - 1, 0)).astype(BF16)
        lo = 0 if b > 0 else 2 * ch
        return (
            dot(above, wk_ref[0, lo : lo + ch])
            + dot(line, wk_ref[1, lo : lo + ch])
            + dot(below, wk_ref[2, lo : lo + ch])
        )

    colf[0] = edge_col(1)
    colf[1] = edge_col(-1)
    place16 = lax.broadcasted_iota(jnp.int32, (16, ch), 0)

    def patch_row(i, carry):
        first = sym[i, 0:16] + jnp.where(place16 == 0, colf[0, pl.ds(i, 1), :], 0.0)
        if cd == 16:
            first = first + jnp.where(place16 == 15, colf[1, pl.ds(i, 1), :], 0.0)
        result[i, 0:16] = first.astype(BF16)
        if cd > 16:
            result[i, cd - 16 : cd] = (
                sym[i, cd - 16 : cd] + jnp.where(place16 == 15, colf[1, pl.ds(i, 1), :], 0.0)
            ).astype(BF16)
        return carry

    lax.fori_loop(1, rd - 1, patch_row, 0, unroll=2)

    for n, q in enumerate((0, stripes - 1)):
        block = (pl.ds(1, rd - 2), pl.ds(q * cr, cr))
        pltpu.make_async_copy(result.at[block], out_ref.at[block], o_sem.at[2]).start()

    take_halo(lambda a: a != 0)
    for a, i in ((1, 0), (-1, rd - 1)):
        edge_row(a, i)
        total = sym[i]
        total = total + jnp.where(along == 0, colf[0, i : i + 1, :], 0.0)
        total = total + jnp.where(along == cd - 1, colf[1, i : i + 1, :], 0.0)
        result[i] = total.astype(BF16)
        pltpu.make_async_copy(result.at[i], out_ref.at[i], o_sem.at[1]).start()

    for k in range(fold):
        @pl.when(jnp.logical_not(l1_target(k)[2]))
        def _():
            pltpu.make_async_copy(lsend.at[k], lsend.at[k], l1_send.at[k]).wait()

        to_row, to_col = col * fold + k, row // fold

        @pl.when(jnp.logical_not(jnp.logical_and(to_row == row, to_col == col)))
        def _():
            src = two.at[pl.ds(0, rd), pl.ds(k * rd, rd)]
            pltpu.make_async_copy(src, src, m_send.at[k]).wait()

    unbend()
    for way in range(2):
        active, to_row, slot = relayed(way)
        for h in range(2):
            for _begin, k, off in segments(h):
                count = steps - 1 if h == 1 else steps
                if k == to_row % fold and count:

                    @pl.when(active)
                    def _():
                        for step in range(count):
                            piece = relay.at[slot, step, off // seg]
                            pltpu.make_async_copy(
                                piece, piece, rl_send.at[slot, step, off // seg]
                            ).wait()

    for t in range(rn - 1):
        for way, (go, slot, _to_row) in enumerate(chain(t)):

            @pl.when(go)
            def _():
                pltpu.make_async_copy(rg.at[slot], rg.at[slot], r_send.at[way, t]).wait()

    others = pl.ds(0, held * (chans - 1))
    if steps > 1:

        @pl.when(away)
        def _():
            got = lg.at[others, pl.ds(1 + cgroups, (steps - 1) * cgroups)]
            pltpu.make_async_copy(got, got, l2_send.at[0]).wait()

    @pl.when(is_home)
    def _():
        pltpu.make_async_copy(lg.at[others], lg.at[others], l2_send.at[0]).wait()
        for d in range(1, chips):
            got = lg.at[pl.ds(0, held)]
            pltpu.make_async_copy(got, got, x_send.at[d - 1]).wait()
            got = lg.at[others, span(0)]
            pltpu.make_async_copy(got, got, e_send.at[d - 1]).wait()

    for n, (a, b) in enumerate(AROUND):

        @pl.when(there(a, b))
        def _():
            piece = hsend.at[n, pl.ds(0, lines(a, b))]
            pltpu.make_async_copy(piece, piece, h_send.at[n]).wait()
    if stripes > 2:
        block = (pl.ds(1, rd - 2), pl.ds(cr, cd - 2 * cr))
        pltpu.make_async_copy(result.at[block], out_ref.at[block], o_sem.at[0]).wait()
    block = pl.ds(0, 2)
    pltpu.make_async_copy(result.at[block], out_ref.at[block], o_sem.at[1]).wait()
    block = (pl.ds(1, rd - 2), pl.ds(0, 2 * cr))
    pltpu.make_async_copy(result.at[block], out_ref.at[block], o_sem.at[2]).wait()


def on_device(
    mesh_shape,
    pair_input,
    alignment_features,
    alignment_mask,
    token_valid,
    left_weight,
    right_weight,
    output_weight,
    gate_weight,
    up_weight,
    down_weight,
    kernel_weight,
):
    rd, cd, ch = pair_input.shape
    sl, tl, aw = alignment_features.shape
    pw = left_weight.shape[1]
    hid = gate_weight.shape[1]
    rn, chans = mesh_shape["row"], mesh_shape["chan"]
    cn = mesh_shape["col"] * chans
    fold = rn // cn
    per = 128 // pw
    cr = min(16, rd)
    depth = rn * sl
    steps = rd // cr
    tall = max(rd, cd, 16)
    half = cd // 2
    seg = min(half, rd)
    subs = rd // seg
    groups, rgroups = rd // per, cd // per
    cuts = min(3, rgroups)
    held = rn // chans
    slots = 1 if cn // chans == 2 else 2
    sizes = (rn, cn, chans, fold, rd, cd, ch, sl, tl, pw, cr)
    operands = (
        alignment_features,
        alignment_mask,
        token_valid.reshape(1, -1),
        left_weight.T,
        right_weight.T,
        pair_input,
        output_weight,
        gate_weight,
        up_weight,
        down_weight,
        kernel_weight.reshape(3, 3 * ch, ch),
    )
    dma = pltpu.SemaphoreType.DMA
    anywhere = pl.BlockSpec(memory_space=pl.ANY)
    return pl.pallas_call(
        functools.partial(block_kernel, sizes),
        out_shape=jax.ShapeDtypeStruct((rd, cd, ch), BF16),
        in_specs=[anywhere] * len(operands),
        out_specs=anywhere,
        scratch_shapes=[
            *[pltpu.VMEM(value.shape, value.dtype) for value in operands],
            dma((len(operands),)),
            pltpu.VMEM((2, sl * tl, 128), F32),
            pltpu.VMEM((tall, ch), F32),
            pltpu.VMEM((fold, groups + 1, sl, 128), BF16),
            pltpu.VMEM((rn, groups + 1, sl, 128), BF16),
            pltpu.VMEM((rn, rgroups + 1, sl, 128), BF16),
            pltpu.VMEM((cd * pw, depth), F32),
            pltpu.VMEM((2, pw // 2 * half, 2 * depth), BF16),
            pltpu.VMEM((2 * depth, cr * pw * 2), BF16),
            pltpu.VMEM((pw * pw, ch), F32),
            pltpu.VMEM((pw // 2 * 128, 2 * ch), BF16),
            pltpu.VMEM((2 * (cr // per) * half, pw // 2 * 128), BF16),
            pltpu.VMEM((rd, cd, ch), F32),
            pltpu.VMEM((128, 128), F32),
            pltpu.VMEM((cr, half, ch), BF16),
            pltpu.VMEM((rd, cd, ch), BF16),
            pltpu.VMEM((cd, rd, ch), BF16),
            pltpu.VMEM((cr * seg, ch), F32),
            pltpu.VMEM((rd, cd, ch), F32),
            pltpu.VMEM((rd + 2, cd, 3 * ch), BF16),
            pltpu.VMEM((2, rd, ch), F32),
            pltpu.VMEM((8, tall, ch), BF16),
            pltpu.VMEM((8, tall, ch), BF16),
            pltpu.VMEM((rd, cd, ch), BF16),
            dma((fold,)),
            dma((held, steps)),
            dma((max(cn // chans - 1, 1),)),
            dma((max(cn // chans - 1, 1),)),
            dma((1,)),
            dma((steps,)),
            dma((2, rn - 1)),
            dma((rn, cuts)),
            dma((fold,)),
            dma((fold, steps, subs)),
            pltpu.VMEM((slots, steps, subs, cr, seg, ch), BF16),
            pltpu.VMEM((max(cn - chans, 1), half // seg, cr, seg, ch), BF16),
            dma((max(cn - chans, 1), half // seg)),
            dma((max(cn - chans, 1), half // seg)),
            dma((slots, steps, subs)),
            dma((slots, steps, subs)),
            dma((8,)),
            dma((8,)),
            dma((3,)),
        ],
        compiler_params=pltpu.CompilerParams(
            collective_id=0, has_side_effects=True, vmem_limit_bytes=44 * 1024 * 1024
        ),
    )(*[pltpu.with_memory_space_constraint(value, pltpu.HBM) for value in operands])


def solution(mesh):
    placed = (
        P(("groups", "row"), ("col", "chan"), None),
        P("row", ("groups", "col", "chan"), None),
        P("row", ("groups", "col", "chan")),
        P("groups"),
        P(),
        P(),
        P(),
        P(),
        P(),
        P(),
        P(),
    )
    return jax.shard_map(
        functools.partial(on_device, dict(mesh.shape)),
        mesh=mesh,
        in_specs=placed,
        out_specs=P(("groups", "row"), ("col", "chan"), None),
        check_vma=False,
    )
```

```python
import functools

import jax
import jax.numpy as jnp
from jax import lax
from jax.experimental import pallas as pl
from jax.experimental.pallas import tpu as pltpu
from jax.sharding import PartitionSpec as P

epsilon = 1e-05
F32, BF16 = jnp.float32, jnp.bfloat16
MESH = pl.DeviceIdType.MESH
AROUND = [(a, b) for a in (-1, 0, 1) for b in (-1, 0, 1) if (a, b) != (0, 0)]


def dot(a, b):
    return jnp.dot(a, b, preferred_element_type=F32)


def block_kernel(sizes, *refs):
    far, (out_ref, *rest) = refs[:11], refs[11:]
    near, (w_sem, *rest) = rest[:11], rest[11:]
    feat_ref, mask_ref, valid_ref, wl_ref, wr_ref = near[:5]
    pair_ref, wo_ref, wg_ref, wu_ref, wd_ref, wk_ref = near[5:]
    (
    proj,
    vrows,
    lsend,
    lg,
    rg,
    rt,
    rq,
    lcat,
    wof,
    w2,
    zs,
    rexp,
    inv,
    ones,
    two,
    mirror,
    mf,
    sym,
    wide,
    colf,
    hsend,
    hrecv,
    result,
    l1_send,
    l1_recv,
    x_send,
    e_send,
    l2_send,
    l2_recv,
    r_send,
    r_recv,
    m_send,
    m_recv,
    relay,
    extra,
    ex_send,
    ex_recv,
    rl_send,
    rl_recv,
    h_send,
    h_recv,
    o_sem,
    ) = rest
    rn, cn, chans, fold, rd, cd, ch, sl, tl, pw, cr = sizes
    row = lax.axis_index("row")
    col = lax.axis_index("col") * chans + lax.axis_index("chan")
    per = 128 // pw
    lgroups, rgroups = rd // per, cd // per
    cuts = min(3, rgroups)
    depth = rn * sl
    steps = rd // cr
    cgroups = cr // per
    half = cd // 2
    seg = min(half, rd)
    subs = rd // seg

    def at(r, c):
        return {"row": r, "col": c // chans, "chan": c % chans}

    def remote(src, dst, ssem, rsem, r, c):
        return pltpu.make_async_remote_copy(
            src_ref=src, dst_ref=dst, send_sem=ssem, recv_sem=rsem,
            device_id=at(r, c), device_id_type=MESH,
        )

    loads = [pltpu.make_async_copy(far[n], near[n], w_sem.at[n]) for n in range(11)]
    for n in (1, 3, 4, 0, 2, 6, 5, 7, 8, 9, 10):
        loads[n].start()
    barrier = pltpu.get_barrier_semaphore()

    def greet(n, carry):
        pl.semaphore_signal(barrier, inc=1, device_id=at(n // cn, n % cn), device_id_type=MESH)
        return carry

    lax.fori_loop(0, rn * cn, greet, 0)
    hrecv[...] = jnp.zeros_like(hrecv)
    for i in (0, rd + 1):
        wide[i] = jnp.zeros((cd, 3 * ch), BF16)

    spread = (
        lax.broadcasted_iota(jnp.int32, (pw, 128), 1) % pw
        == lax.broadcasted_iota(jnp.int32, (pw, 128), 0)
    ).astype(F32).astype(BF16)
    for n in (1, 3, 4):
        loads[n].wait()
    mask = mask_ref[...].astype(F32).astype(BF16)
    spots = tl // per
    token_of = (
        lax.broadcasted_iota(jnp.int32, (tl, spots * 128), 1) // pw
        == lax.broadcasted_iota(jnp.int32, (tl, spots * 128), 0)
    ).astype(F32).astype(BF16)
    wide_mask = dot(mask, token_of)
    tiles = [
        lax.dot_general(
            w_ref[...], spread, (((0,), (0,)), ((), ())), preferred_element_type=F32
        ).astype(BF16)
        for w_ref in (wl_ref, wr_ref)
    ]
    loads[0].wait()
    feats = feat_ref[...].reshape(sl * tl, feat_ref.shape[2])
    lane_of = lax.broadcasted_iota(jnp.int32, (sl, 128), 1) // pw

    def project(n):
        proj[n] = dot(feats, tiles[n])
        parts = []
        for g in range(spots):
            got = proj[n, pl.ds(g * per, sl, stride=tl), :]
            for t in range(1, per):
                other = proj[n, pl.ds(g * per + t, sl, stride=tl), :]
                got = jnp.where(lane_of == t, other, got)
            parts.append((got * wide_mask[:, g * 128 : (g + 1) * 128]).astype(BF16))
        return parts

    left = project(0)
    for k in range(fold):
        for g in range(lgroups):
            lsend[k, 1 + g] = left[k * lgroups + g]
        lsend[k, 0] = jnp.zeros((sl, 128), BF16)
        lsend[k, 0, :, 0:rd] = mask[:, k * rd : (k + 1) * rd]
    def project_right():
        right = project(1)
        for g in range(rgroups):
            rg[row, 1 + g] = right[g]
        rg[row, 0] = jnp.zeros((sl, 128), BF16)
        rg[row, 0, :, 0:tl] = mask

    early = row < rn // 2

    @pl.when(early)
    def _():
        project_right()


    pl.semaphore_wait(barrier, rn * cn)

    def span(n):
        if isinstance(n, int) and n == 0:
            return pl.ds(0, cgroups + 1)
        return pl.ds(1 + n * cgroups, cgroups)

    core, chip = col % chans, col // chans
    held = rn // chans
    home = row // fold // chans
    is_home = chip == home

    def l1_target(k):
        to_row, to_col = col * fold + k, chip * chans + row % chans
        return to_row, to_col, jnp.logical_and(to_row == row, to_col == col)

    def send_left(n):
        for k in range(fold):
            to_row, to_col, mine = l1_target(k)
            slot = row // chans
            src, dst = lsend.at[k, span(n)], lg.at[row, span(n)]

            @pl.when(mine)
            def _():
                pltpu.make_async_copy(src, dst, l1_recv.at[slot, n]).start()

            @pl.when(jnp.logical_not(mine))
            def _():
                remote(src, dst, l1_send.at[k], l1_recv.at[slot, n], to_row, to_col).start()

    chips = cn // chans

    def spread_left(i, n, at_home):
        m = (row // chans + i) % held
        first = isinstance(n, int) and n == 0
        piece = lg.at[m * chans + core, span(n)]
        pltpu.make_async_copy(piece, piece, l1_recv.at[m, n]).wait()
        if at_home:
            for d in range(1, chips):
                there_chip = (chip + d) % chips * chans
                remote(
                    piece, piece, x_send.at[d - 1], l1_recv.at[m, n], row, there_chip + core
                ).start()
                for e in range(1, chans if first else 0):
                    remote(
                        piece, piece, e_send.at[d - 1], l2_recv.at[n],
                        row, there_chip + (core + e) % chans,
                    ).start()
        for e in range(1, chans if at_home or not first else 0):
            remote(
                piece, piece, l2_send.at[0], l2_recv.at[n],
                row, chip * chans + (core + e) % chans,
            ).start()

    def take_left(n):
        got = lg.at[pl.ds(0, held * (chans - 1)), span(n)]
        pltpu.make_async_copy(got, got, l2_recv.at[n]).wait()

    send_left(0)

    @pl.when(jnp.logical_not(early))
    def _():
        project_right()

    def chain(t):
        low, high = jnp.maximum(row - t, 0), jnp.minimum(row + t, rn - 1)
        ups = jnp.logical_and(row - t >= 0, row + 1 < rn)
        downs = jnp.logical_and(row + t < rn, row >= 1)
        return (ups, low, row + 1), (downs, high, row - 1)

    quarter = max(rgroups // 4, 1)
    early_pieces = [
        pl.ds(1 + e * quarter, quarter) if e else pl.ds(0, 1 + quarter)
        for e in range(rgroups // 2 // quarter)
    ]
    pieces = early_pieces + [pl.ds(1 + rgroups // 2, rgroups - rgroups // 2)]

    upward = chip < chips // 2

    def pass_on(urgent, later):
        for way, (go, slot, to_row) in enumerate(chain(0)):

            @pl.when(jnp.logical_and(go, upward == (urgent == (way == 0))))
            def _():
                for e in cut_range(later):
                    part_of = rg.at[slot, pieces[e]]
                    remote(
                        part_of, part_of, r_send.at[way, 0], r_recv.at[slot, e], to_row, col
                    ).start()

    def cut_range(later):
        return range(cuts - 1, cuts) if later else range(cuts - 1)

    pass_on(True, False)
    pass_on(False, False)
    pass_on(True, True)
    for n in range(1, steps):
        send_left(n)

    loads[2].wait()
    tokens = valid_ref.shape[1]
    valid = valid_ref[...].astype(F32)

    def as_rows(first, count):
        hit = lax.broadcasted_iota(jnp.int32, (count, tokens), 1) == first + (
            lax.broadcasted_iota(jnp.int32, (count, tokens), 0)
        )
        chosen = jnp.where(hit, jnp.broadcast_to(valid, (count, tokens)), 0.0).astype(BF16)
        return dot(chosen, jnp.ones((tokens, ch), BF16))

    vrows[0:rd] = as_rows(row * rd, rd)
    valid_cols = as_rows(col * cd, cd)

    loads[6].wait()
    wof[...] = wo_ref[...].astype(F32)
    w2[...] = jnp.zeros_like(w2)
    for q in range(pw):
        values = wof[pl.ds(q, pw, stride=pw), :].astype(BF16)
        for i in range(2):
            begin = q // 2 * 128 + (q % 2 * 2 + i) * pw
            w2[begin : begin + pw, i * ch : (i + 1) * ch] = values

    def hop(t, way, later):
        there_is, slot = (
            (row - t - 1 >= 0, jnp.maximum(row - t - 1, 0)),
            (row + t + 1 < rn, jnp.minimum(row + t + 1, rn - 1)),
        )[way]
        for e in cut_range(later):
            piece = pieces[e]

            @pl.when(there_is)
            def _():
                part_of = rg.at[slot, piece]
                pltpu.make_async_copy(part_of, part_of, r_recv.at[slot, e]).wait()

            if t + 1 < rn - 1:
                go, _slot, to_row = chain(t + 1)[way]

                @pl.when(go)
                def _():
                    part_of = rg.at[slot, piece]
                    remote(
                        part_of, part_of, r_send.at[way, t + 1], r_recv.at[slot, e],
                        to_row, col,
                    ).start()

    def hops(first, last, urgent, later=False):

        @pl.when(upward if urgent else jnp.logical_not(upward))
        def _():
            for t in range(first, last):
                hop(t, 0, later)

        @pl.when(jnp.logical_not(upward) if urgent else upward)
        def _():
            for t in range(first, last):
                hop(t, 1, later)

    ends = jnp.logical_or(row == 0, row == rn - 1)
    inner = jnp.logical_not(ends)
    away = jnp.logical_not(is_home)

    @pl.when(is_home)
    def _():
        spread_left(0, 0, True)

    @pl.when(is_home)
    def _():
        for i in range(1, held):
            spread_left(i, 0, True)

    @pl.when(jnp.logical_and(away, ends))
    def _():
        for i in range(held):
            spread_left(i, 0, False)

    hops(0, 1, True)
    @pl.when(ends)
    def _():
        pass_on(False, True)


    hops(0, 1, False)

    hops(1, rn - 1, True)

    @pl.when(jnp.logical_and(away, inner))
    def _():
        for i in range(held):
            spread_left(i, 0, False)

    @pl.when(is_home)
    def _():
        for n in range(1, steps):
            for i in range(held):
                spread_left(i, n, True)

    @pl.when(is_home)
    def _():
        hops(0, 1, True, True)

    hops(1, rn - 1, False)

    @pl.when(inner)
    def _():
        pass_on(False, True)

    @pl.when(away)
    def _():
        hops(0, 1, True, True)

    take_left(0)
    left_mask = lg[:, 0].astype(F32).reshape(depth, 128)
    right_mask = rg[:, 0].astype(F32).reshape(depth, 128)
    counts = dot(right_mask.T.astype(BF16), left_mask.astype(BF16))
    inv[...] = 1.0 / jnp.maximum(counts, 1.0)

    def prepare(h):
        for g in range(h * rgroups // 2, (h + 1) * rgroups // 2):
            slab = rg[:, 1 + g].astype(F32).reshape(depth, 128)
            rt[g * 128 : (g + 1) * 128, :] = slab.T
        for q in range(pw):
            rq[h, q // 2 * half : (q // 2 + 1) * half, q % 2 * depth : (q % 2 + 1) * depth] = rt[
                pl.ds(h * half * pw + q, half, stride=pw), :
            ].astype(BF16)
        inverse = inv[h * half : (h + 1) * half]
        for i in range(rd):
            rexp[i, h * half : (h + 1) * half] = jnp.broadcast_to(
                inverse[:, i : i + 1], (half, ch)
            )

    prepare(0)

    for n in (5, 7, 8, 9, 10):
        loads[n].wait()

    lag = 0

    slots = 1 if chips == 2 else 2
    final = steps - 1

    def segments(h):
        found = []
        for begin in range(h * half, (h + 1) * half, seg):
            found.append((begin, begin // rd, begin % rd))
        return found

    def send_mirror(h, step):
        for g, (begin, k, off) in enumerate(segments(h)):
            to_row, to_col = col * fold + k, row // fold
            mine = jnp.logical_and(to_row == row, to_col == col)
            across = to_col // chans != chip
            at_end = jnp.logical_or(to_row == 0, to_row == rn - 1)
            turned = jnp.logical_and(across, at_end)
            if h == 1:
                turned = jnp.logical_and(turned, step != final)
            bent = jnp.logical_and(across, jnp.logical_not(at_end))
            bent = bent & inner & jnp.logical_not(upward)
            bent = jnp.logical_and(bent, step == 0) if h == 1 else False
            sub = off // seg
            src = two.at[pl.ds(step * cr, cr), pl.ds(begin, seg)]
            dst = mirror.at[pl.ds(row % fold * rd + step * cr, cr), pl.ds(off, seg)]
            rsem = m_recv.at[row % fold, step, sub]
            ssem = m_send.at[k]

            @pl.when(mine)
            def _():
                pltpu.make_async_copy(src, dst, rsem).start()

            @pl.when(turned)
            def _():
                slot = jnp.where(to_row == 0, 0, slots - 1)
                remote(
                    src, relay.at[slot, step, sub], ssem, rl_recv.at[slot, step, sub],
                    row, to_col,
                ).start()

            if h == 1:

                @pl.when(bent)
                def _():
                    slot = (col + 2 * cn - (to_col // chans + 1) * chans) % cn
                    remote(
                        src, extra.at[slot, g], ssem, ex_recv.at[slot, g], row, to_col
                    ).start()

            @pl.when(jnp.logical_not(mine | turned | bent))
            def _():
                remote(src, dst, ssem, rsem, to_row, to_col).start()

    def relayed(way):
        to_row = (0, rn - 1)[way]
        active = jnp.logical_and(col == row // fold, to_row // fold // chans != chip)
        return active, to_row, way % slots

    def forward(h, step):
        for way in range(2):
            active, to_row, slot = relayed(way)
            if h == 1:
                active = jnp.logical_and(active, step != final)
            for _begin, k, off in segments(h):
                if k == to_row % fold:
                    sub = off // seg

                    @pl.when(active)
                    def _():
                        piece = relay.at[slot, step, sub]
                        pltpu.make_async_copy(piece, piece, rl_recv.at[slot, step, sub]).wait()
                        remote(
                            piece,
                            mirror.at[pl.ds(row % fold * rd + step * cr, cr), pl.ds(off, seg)],
                            rl_send.at[slot, step, sub],
                            m_recv.at[row % fold, step, sub], to_row, col,
                        ).start()

    def bend():
        for slot in range(cn - chans):
            from_col = ((chip + 1) * chans + slot) % cn
            for g, (_begin, k, off) in enumerate(segments(1)):
                to_row = from_col * fold + k
                active = (col == row // fold) & inner & (to_row != 0) & (to_row != rn - 1)
                active = active & (from_col // chans >= chips // 2)

                @pl.when(active)
                def _():
                    piece = extra.at[slot, g]
                    pltpu.make_async_copy(piece, piece, ex_recv.at[slot, g]).wait()
                    remote(
                        piece, mirror.at[pl.ds(row % fold * rd, cr), pl.ds(off, seg)],
                        ex_send.at[slot, g], m_recv.at[row % fold, 0, off // seg],
                        to_row, col,
                    ).start()

    def unbend():
        for slot in range(cn - chans):
            from_col = ((chip + 1) * chans + slot) % cn
            for g, (_begin, k, _off) in enumerate(segments(1)):
                to_row = from_col * fold + k
                active = (col == row // fold) & inner & (to_row != 0) & (to_row != rn - 1)
                active = active & (from_col // chans >= chips // 2)

                @pl.when(active)
                def _():
                    piece = extra.at[slot, g]
                    pltpu.make_async_copy(piece, piece, ex_send.at[slot, g]).wait()

    low_lanes = lax.broadcasted_iota(jnp.int32, (depth, 128), 1) < 64

    def serve(step):
        for t in range(rn - 1):

            @pl.when(step == jnp.where(ends, steps - 1, min(t, steps - 1)))
            def _():
                for way in (0, 1):
                    if t:
                        hop(t, way, True)
                    else:

                        @pl.when(upward == (way == 1))
                        def _():
                            hop(0, way, True)

        @pl.when(jnp.logical_and(away, step + 1 < steps))
        def _():
            for i in range(held):
                spread_left(i, step + 1, False)

        @pl.when(step > 0)
        def _():
            take_left(step)

    def one_step(h, step):
        lo = h * half
        if h == 0:

            @pl.when(inner & (step > 0))
            def _():
                forward(h, step)

            serve(step)

            @pl.when(inner & (step == 0))
            def _():
                forward(h, step)

        else:

            @pl.when(inner)
            def _():
                forward(h, step)

            @pl.when(step == min(2, steps - 1))
            def _():
                bend()


        if h and lag:

            @pl.when(step < lag)
            def _():
                forward(h - 1, steps - lag + step)

        for g in range(cgroups):
            slab = lg[:, 1 + step * cgroups + g].astype(F32).reshape(depth, 128)
            turned = pltpu.roll(slab, 64, 1)
            for i, (first, second) in enumerate(((slab, turned), (turned, slab))):
                at_lane = (g * 2 + i) * 128
                lcat[0:depth, at_lane : at_lane + 128] = jnp.where(low_lanes, first, 0.0).astype(BF16)
                lcat[depth : 2 * depth, at_lane : at_lane + 128] = jnp.where(
                    low_lanes, 0.0, second
                ).astype(BF16)
        for g in range(cgroups):
            z = dot(rq[h], lcat[:, g * 256 : (g + 1) * 256]).astype(BF16)
            for i in range(2):
                for q in range(pw // 2):
                    begin = (i * cgroups + g) * half
                    zs[begin : begin + half, q * 128 : (q + 1) * 128] = z[
                        q * half : (q + 1) * half, i * 128 : (i + 1) * 128
                    ]
        update = dot(zs[...], w2[...])
        for g in range(cgroups):
            for i in range(per):
                at_row = step * cr + g * per + i
                begin = (i // 2 * cgroups + g) * half
                add = update[begin : begin + half, i % 2 * ch : (i % 2 + 1) * ch]
                add = add * rexp[at_row, lo : lo + half]
                ones[g * per + i] = (pair_ref[at_row, lo : lo + half].astype(F32) + add).astype(BF16)
        values = ones[...].reshape(cr * half, ch).astype(F32)
        centre = jnp.mean(values, axis=-1, keepdims=True)
        shifted = values - centre
        var = jnp.mean(jnp.square(shifted), axis=-1, keepdims=True)
        normed = (shifted * lax.rsqrt(var + epsilon)).astype(BF16)
        gate = dot(normed, wg_ref[...])
        up = dot(normed, wu_ref[...])
        halved = gate * 0.5
        hidden = ((halved + halved * jnp.tanh(halved)) * up).astype(BF16)
        done = (values + dot(hidden, wd_ref[...])).astype(BF16)
        two[pl.ds(step * cr, cr), lo : lo + half] = done.reshape(cr, half, ch)
        send_mirror(h, step)

        @pl.when(ends)
        def _():
            forward(h, step)


    def run(h):
        def body(step, carry):
            one_step(h, step)
            return carry

        lax.fori_loop(0, steps, body, 0)

    run(0)
    prepare(1)
    run(1)
    for step in range(steps - lag, steps):
        forward(1, step)

    stripes = cd // cr
    place = lax.broadcasted_iota(jnp.int32, (cr, ch), 0)

    def take_mirror(sub, q):
        begin = q * cr
        k, step = begin // rd, begin % rd // cr
        top = sub * seg
        piece = mirror.at[pl.ds(begin, cr), pl.ds(top, seg)]
        pltpu.make_async_copy(piece, piece, m_recv.at[k, step, sub]).wait()
        mf[0 : cr * seg] = (
            mirror[begin : begin + cr, top : top + seg].astype(F32).reshape(cr * seg, ch)
        )
        some_cols = valid_cols[begin : begin + cr]

        def one_row(i, carry):
            other = mf[pl.ds(i - top, cr, stride=seg), :]
            half_sum = (two[i, begin : begin + cr].astype(F32) + other) * 0.5
            sym[i, begin : begin + cr] = half_sum
            masked = half_sum * some_cols * vrows[pl.ds(i, 1), :]
            wide[i + 1, begin : begin + cr, ch : 2 * ch] = masked.astype(BF16)
            before = colf[1, pl.ds(i, 1), :] if q else 0.0
            wide[i + 1, begin : begin + cr, 0:ch] = jnp.where(
                place == 0, before, pltpu.roll(masked, 1, 0)
            ).astype(BF16)
            if q:
                earlier = wide[i + 1, begin - cr : begin, ch : 2 * ch].astype(F32)
                wide[i + 1, begin - cr : begin, 2 * ch : 3 * ch] = jnp.where(
                    place == cr - 1, masked[0:1], pltpu.roll(earlier, cr - 1, 0)
                ).astype(BF16)
            else:
                colf[0, pl.ds(i, 1), :] = masked[0:1]
            if q == stripes - 1:
                wide[i + 1, begin : begin + cr, 2 * ch : 3 * ch] = jnp.where(
                    place == cr - 1, 0.0, pltpu.roll(masked, cr - 1, 0)
                ).astype(BF16)
            colf[1, pl.ds(i, 1), :] = masked[cr - 1 : cr]
            return carry

        lax.fori_loop(top, top + seg, one_row, 0, unroll=8)

    top_rows = seg // 2 if subs > 1 else 0
    blocks = [(0, top_rows)] if top_rows else []
    while (blocks[-1][1] if blocks else 0) < rd:
        first = blocks[-1][1] if blocks else 0
        blocks.append((first, min(first + 32, rd)))

    def conv_block(q, first, last):
        begin = q * cr
        count = last - first
        total = sym[first:last, begin : begin + cr].reshape(count * cr, ch)
        for a in range(3):
            window = wide[first + a : last + a, begin : begin + cr]
            total = total + dot(window.reshape(count * cr, 3 * ch), wk_ref[a])
        total = total.reshape(count, cr, ch)
        result[first:last, begin : begin + cr] = total.astype(BF16)
        if q in (0, stripes - 1):
            sym[first:last, begin : begin + cr] = total
        else:
            if first == 0:
                sym[0, begin : begin + cr] = total[0]
            if last == rd:
                sym[rd - 1, begin : begin + cr] = total[count - 1]

    def conv(q):
        for first, last in blocks[1 if top_rows else 0 :]:
            conv_block(q, first, last)
        if 0 < q < stripes - 1:
            middle(q).start()

    def middle(q):
        block = (pl.ds(1, rd - 2), pl.ds(q * cr, cr))
        return pltpu.make_async_copy(result.at[block], out_ref.at[block], o_sem.at[0])

    def there(a, b):
        r, c = row + a, col + b
        return jnp.logical_and(
            jnp.logical_and(r >= 0, r < rn), jnp.logical_and(c >= 0, c < cn)
        )

    def lines(a, b):
        return cd if b == 0 else (rd if a == 0 else 16)

    def send_halo(ready):
        for n, (a, b) in enumerate(AROUND):
            if not ready(a, b):
                continue
            size = lines(a, b)
            side = 0 if b < 0 else 1
            if b == 0:
                hsend[n, 0:cd] = wide[1 if a < 0 else rd, :, ch : 2 * ch]
            elif a == 0:
                hsend[n, 0:rd] = colf[side].astype(BF16)
            else:
                corner = colf[side, 0:1] if a < 0 else colf[side, rd - 1 : rd]
                hsend[n, 0:16] = jnp.broadcast_to(corner, (16, ch)).astype(BF16)

            @pl.when(there(a, b))
            def _():
                remote(
                    hsend.at[n, pl.ds(0, size)], hrecv.at[n, pl.ds(0, size)], h_send.at[n],
                    h_recv.at[n], row + a, col + b,
                ).start()

    done = 0
    for sub in range(subs):
        for q in range(stripes):
            take_mirror(sub, q)
            if sub == subs - 1 and q == 0:
                send_halo(lambda a, b: b < 0 and a >= 0)
            if sub == 0 and top_rows and q:
                conv_block(q - 1, 0, top_rows)
            if sub == subs - 1 and 0 < q < stripes - 2:
                conv(q - 1)
                done = q
        if sub == 0 and subs > 1:
            send_halo(lambda a, b: a < 0)
        if sub == 0 and top_rows:
            conv_block(stripes - 1, 0, top_rows)

    send_halo(lambda a, b: not (a < 0 and subs > 1) and not (b < 0 and a >= 0))

    for q in range(done, stripes):
        conv(q)

    def take_halo(wanted):
        for n, (a, b) in enumerate(AROUND):
            if wanted(a):

                @pl.when(there(-a, -b))
                def _():
                    piece = hrecv.at[n, pl.ds(0, lines(a, b))]
                    pltpu.make_async_copy(piece, piece, h_recv.at[n]).wait()

    take_halo(lambda a: a == 0)

    slot_of = {direction: n for n, direction in enumerate(AROUND)}
    along = lax.broadcasted_iota(jnp.int32, (cd, ch), 0)
    down = lax.broadcasted_iota(jnp.int32, (rd, ch), 0)

    def edge_row(a, i):
        line = hrecv[slot_of[(a, 0)], 0:cd]
        centre = line.astype(F32)
        before = hrecv[slot_of[(a, 1)], 0:16].astype(F32)[0:1]
        after = hrecv[slot_of[(a, -1)], 0:16].astype(F32)[0:1]
        lefts = jnp.where(along == 0, before, pltpu.roll(centre, 1, 0)).astype(BF16)
        rights = jnp.where(along == cd - 1, after, pltpu.roll(centre, cd - 1, 0)).astype(BF16)
        w = 0 if a > 0 else 2
        sym[i] = sym[i] + (
            dot(lefts, wk_ref[w, 0:ch])
            + dot(line, wk_ref[w, ch : 2 * ch])
            + dot(rights, wk_ref[w, 2 * ch : 3 * ch])
        )

    def edge_col(b):
        line = hrecv[slot_of[(0, b)], 0:rd]
        centre = line.astype(F32)
        above = jnp.where(down == 0, 0.0, pltpu.roll(centre, 1, 0)).astype(BF16)
        below = jnp.where(down == rd - 1, 0.0, pltpu.roll(centre, rd - 1, 0)).astype(BF16)
        lo = 0 if b > 0 else 2 * ch
        return (
            dot(above, wk_ref[0, lo : lo + ch])
            + dot(line, wk_ref[1, lo : lo + ch])
            + dot(below, wk_ref[2, lo : lo + ch])
        )

    colf[0] = edge_col(1)
    colf[1] = edge_col(-1)
    place16 = lax.broadcasted_iota(jnp.int32, (16, ch), 0)

    def patch_row(i, carry):
        first = sym[i, 0:16] + jnp.where(place16 == 0, colf[0, pl.ds(i, 1), :], 0.0)
        if cd == 16:
            first = first + jnp.where(place16 == 15, colf[1, pl.ds(i, 1), :], 0.0)
        result[i, 0:16] = first.astype(BF16)
        if cd > 16:
            result[i, cd - 16 : cd] = (
                sym[i, cd - 16 : cd] + jnp.where(place16 == 15, colf[1, pl.ds(i, 1), :], 0.0)
            ).astype(BF16)
        return carry

    lax.fori_loop(1, rd - 1, patch_row, 0, unroll=2)

    for n, q in enumerate((0, stripes - 1)):
        block = (pl.ds(1, rd - 2), pl.ds(q * cr, cr))
        pltpu.make_async_copy(result.at[block], out_ref.at[block], o_sem.at[2]).start()

    take_halo(lambda a: a != 0)
    for a, i in ((1, 0), (-1, rd - 1)):
        edge_row(a, i)
        total = sym[i]
        total = total + jnp.where(along == 0, colf[0, i : i + 1, :], 0.0)
        total = total + jnp.where(along == cd - 1, colf[1, i : i + 1, :], 0.0)
        result[i] = total.astype(BF16)
        pltpu.make_async_copy(result.at[i], out_ref.at[i], o_sem.at[1]).start()

    for k in range(fold):
        @pl.when(jnp.logical_not(l1_target(k)[2]))
        def _():
            pltpu.make_async_copy(lsend.at[k], lsend.at[k], l1_send.at[k]).wait()

        to_row, to_col = col * fold + k, row // fold

        @pl.when(jnp.logical_not(jnp.logical_and(to_row == row, to_col == col)))
        def _():
            src = two.at[pl.ds(0, rd), pl.ds(k * rd, rd)]
            pltpu.make_async_copy(src, src, m_send.at[k]).wait()

    unbend()
    for way in range(2):
        active, to_row, slot = relayed(way)
        for h in range(2):
            for _begin, k, off in segments(h):
                count = steps - 1 if h == 1 else steps
                if k == to_row % fold and count:

                    @pl.when(active)
                    def _():
                        for step in range(count):
                            piece = relay.at[slot, step, off // seg]
                            pltpu.make_async_copy(
                                piece, piece, rl_send.at[slot, step, off // seg]
                            ).wait()

    for t in range(rn - 1):
        for way, (go, slot, _to_row) in enumerate(chain(t)):

            @pl.when(go)
            def _():
                pltpu.make_async_copy(rg.at[slot], rg.at[slot], r_send.at[way, t]).wait()

    others = pl.ds(0, held * (chans - 1))
    if steps > 1:

        @pl.when(away)
        def _():
            got = lg.at[others, pl.ds(1 + cgroups, (steps - 1) * cgroups)]
            pltpu.make_async_copy(got, got, l2_send.at[0]).wait()

    @pl.when(is_home)
    def _():
        pltpu.make_async_copy(lg.at[others], lg.at[others], l2_send.at[0]).wait()
        for d in range(1, chips):
            got = lg.at[pl.ds(0, held)]
            pltpu.make_async_copy(got, got, x_send.at[d - 1]).wait()
            got = lg.at[others, span(0)]
            pltpu.make_async_copy(got, got, e_send.at[d - 1]).wait()

    for n, (a, b) in enumerate(AROUND):

        @pl.when(there(a, b))
        def _():
            piece = hsend.at[n, pl.ds(0, lines(a, b))]
            pltpu.make_async_copy(piece, piece, h_send.at[n]).wait()
    if stripes > 2:
        block = (pl.ds(1, rd - 2), pl.ds(cr, cd - 2 * cr))
        pltpu.make_async_copy(result.at[block], out_ref.at[block], o_sem.at[0]).wait()
    block = pl.ds(0, 2)
    pltpu.make_async_copy(result.at[block], out_ref.at[block], o_sem.at[1]).wait()
    block = (pl.ds(1, rd - 2), pl.ds(0, 2 * cr))
    pltpu.make_async_copy(result.at[block], out_ref.at[block], o_sem.at[2]).wait()


def on_device(
    mesh_shape,
    pair_input,
    alignment_features,
    alignment_mask,
    token_valid,
    left_weight,
    right_weight,
    output_weight,
    gate_weight,
    up_weight,
    down_weight,
    kernel_weight,
):
    rd, cd, ch = pair_input.shape
    sl, tl, aw = alignment_features.shape
    pw = left_weight.shape[1]
    hid = gate_weight.shape[1]
    rn, chans = mesh_shape["row"], mesh_shape["chan"]
    cn = mesh_shape["col"] * chans
    fold = rn // cn
    per = 128 // pw
    cr = min(16, rd)
    depth = rn * sl
    steps = rd // cr
    tall = max(rd, cd, 16)
    half = cd // 2
    seg = min(half, rd)
    subs = rd // seg
    groups, rgroups = rd // per, cd // per
    cuts = min(3, rgroups)
    held = rn // chans
    slots = 1 if cn // chans == 2 else 2
    sizes = (rn, cn, chans, fold, rd, cd, ch, sl, tl, pw, cr)
    operands = (
        alignment_features,
        alignment_mask,
        token_valid.reshape(1, -1),
        left_weight.T,
        right_weight.T,
        pair_input,
        output_weight,
        gate_weight,
        up_weight,
        down_weight,
        kernel_weight.reshape(3, 3 * ch, ch),
    )
    dma = pltpu.SemaphoreType.DMA
    anywhere = pl.BlockSpec(memory_space=pl.ANY)
    return pl.pallas_call(
        functools.partial(block_kernel, sizes),
        out_shape=jax.ShapeDtypeStruct((rd, cd, ch), BF16),
        in_specs=[anywhere] * len(operands),
        out_specs=anywhere,
        scratch_shapes=[
            *[pltpu.VMEM(value.shape, value.dtype) for value in operands],
            dma((len(operands),)),
            pltpu.VMEM((2, sl * tl, 128), F32),
            pltpu.VMEM((tall, ch), F32),
            pltpu.VMEM((fold, groups + 1, sl, 128), BF16),
            pltpu.VMEM((rn, groups + 1, sl, 128), BF16),
            pltpu.VMEM((rn, rgroups + 1, sl, 128), BF16),
            pltpu.VMEM((cd * pw, depth), F32),
            pltpu.VMEM((2, pw // 2 * half, 2 * depth), BF16),
            pltpu.VMEM((2 * depth, cr * pw * 2), BF16),
            pltpu.VMEM((pw * pw, ch), F32),
            pltpu.VMEM((pw // 2 * 128, 2 * ch), BF16),
            pltpu.VMEM((2 * (cr // per) * half, pw // 2 * 128), BF16),
            pltpu.VMEM((rd, cd, ch), F32),
            pltpu.VMEM((128, 128), F32),
            pltpu.VMEM((cr, half, ch), BF16),
            pltpu.VMEM((rd, cd, ch), BF16),
            pltpu.VMEM((cd, rd, ch), BF16),
            pltpu.VMEM((cr * seg, ch), F32),
            pltpu.VMEM((rd, cd, ch), F32),
            pltpu.VMEM((rd + 2, cd, 3 * ch), BF16),
            pltpu.VMEM((2, rd, ch), F32),
            pltpu.VMEM((8, tall, ch), BF16),
            pltpu.VMEM((8, tall, ch), BF16),
            pltpu.VMEM((rd, cd, ch), BF16),
            dma((fold,)),
            dma((held, steps)),
            dma((max(cn // chans - 1, 1),)),
            dma((max(cn // chans - 1, 1),)),
            dma((1,)),
            dma((steps,)),
            dma((2, rn - 1)),
            dma((rn, cuts)),
            dma((fold,)),
            dma((fold, steps, subs)),
            pltpu.VMEM((slots, steps, subs, cr, seg, ch), BF16),
            pltpu.VMEM((max(cn - chans, 1), half // seg, cr, seg, ch), BF16),
            dma((max(cn - chans, 1), half // seg)),
            dma((max(cn - chans, 1), half // seg)),
            dma((slots, steps, subs)),
            dma((slots, steps, subs)),
            dma((8,)),
            dma((8,)),
            dma((3,)),
        ],
        compiler_params=pltpu.CompilerParams(
            collective_id=0, has_side_effects=True, vmem_limit_bytes=44 * 1024 * 1024
        ),
    )(*[pltpu.with_memory_space_constraint(value, pltpu.HBM) for value in operands])


def solution(mesh):
    placed = (
        P(("groups", "row"), ("col", "chan"), None),
        P("row", ("groups", "col", "chan"), None),
        P("row", ("groups", "col", "chan")),
        P("groups"),
        P(),
        P(),
        P(),
        P(),
        P(),
        P(),
        P(),
    )
    return jax.shard_map(
        functools.partial(on_device, dict(mesh.shape)),
        mesh=mesh,
        in_specs=placed,
        out_specs=P(("groups", "row"), ("col", "chan"), None),
        check_vma=False,
    )
```
